256 devices in a mesh: dp: 8 (over z_lo, y), expert: 32 (over z_hi, x, core).
Axes of the slice: x: 4, y: 4, z: 8 (z_hi: 4, z_lo: 2; z = z_hi * 2 + z_lo), core: 2. Of those that a mesh axis runs over, the one named last changes fastest.
Arguments:
- cell_rows: bfloat16 [2, 32768, 1024], P(None, ('dp', 'expert')), may hold values from -24 to 24
- cotangent: bfloat16 [2, 32768, 1024], P(None, ('dp', 'expert')), may hold values from -0.75 to 0.75
- cluster_ids: int32 [2, 32768, 1], P(None, ('dp', 'expert')), may hold values from 0 to 31; in each aligned block of 128 rows (0 to 127, 128 to 255, ..., all dimensions but the last counted through in order) at most 8 rows name the same one
- enc_weight: bfloat16 [1024, 1024], replicated, may hold values from -0.1875 to 0.1875
- up_weight: bfloat16 [32, 1024, 2048], P('expert'), may hold values from -0.1875 to 0.1875
- down_weight: bfloat16 [32, 1024, 2048], P('expert'), may hold values from -0.125 to 0.125
Outputs:
- enc_grad: float32 [1024, 1024], P(('dp', 'expert'))
- up_grad: bfloat16 [32, 1024, 2048], P('expert', 'dp')
- down_grad: bfloat16 [32, 1024, 2048], P('expert', 'dp')
The draws below stay inside these ranges and needn't reach their ends.
Inputs may be any that keep to these rules, and one draw needn't show every extreme that they name: `cluster_ids`: in each micro-batch the 128 rows of one device name one cluster at most 8 times, a bound that some block reaches.
All inputs are finite; a program needn't handle non-finite values.
Results may differ from the reference program's by a relative error of at most 0.014.
Values may be sent and summed in bfloat16 or wider, within the bound.
A program may use at most 128 MiB of HBM per device.

```python
import math
import jax
import jax.numpy as jnp
import numpy as np
from jax import lax

D = 1024
H = 2048
MICRO = 2
MB_ROWS = 128
CLUSTERS = 32
CAP = 8
TOKENS_MB = 32768
N_DP = 8
N_EXPERT = 32


def with_spikes(values, own_key, source, target, blocks, factor):
    def block_of(position):
        return (jnp.arange(values.shape[position]) // (values.shape[position] // blocks)).reshape((-1,) + (1,) * (values.ndim - 1 - position))

    one_side = jax.random.permutation(own_key, blocks)[block_of(target)]
    other_side = (block_of(target) + blocks // 2) % blocks
    return jnp.where((block_of(source) == one_side) | (block_of(source) == other_side), factor * values, values)


def block_levels(key, shape, pieces, smallest, top_value):
    gain = 1.0
    for axis_at, parts in pieces:
        draws = jax.random.uniform(jax.random.fold_in(jax.random.fold_in(key, 6), axis_at), (parts,), jnp.float32, smallest / len(pieces), top_value / len(pieces))
        gain = gain * jnp.repeat(jnp.exp(draws), shape[axis_at] // parts).reshape((-1,) + (1,) * (len(shape) - 1 - axis_at))
    return gain


def deal_out(stream_key, own, number, rows, count, top, bound, lean):
    order = jax.random.permutation(stream_key, count)
    packed, ordinary = shares(count, rows * top, bound, lean, True), shares(count, rows * top, bound, lean, False)
    places = jnp.arange(count)

    def named(tallies, offset_by):
        used = int((tallies > 0).sum())
        fixed = max(1, used // 4)
        passed = fixed + (places - fixed + offset_by * (used - fixed)) % max(1, count - fixed)
        return jnp.zeros((count,), jnp.int32).at[order[jnp.where(places < fixed, places, passed)]].set(jnp.asarray(tallies, jnp.int32))

    tallies = jnp.where(number % 4 == 0, named(packed, number // 4), named(ordinary, number - number // 4 - 1))
    mixed = jax.random.permutation(jax.random.fold_in(own, 3), count)
    giver, sink = mixed[0:count // 2 * 2:2], mixed[1:count // 2 * 2:2]
    room = jnp.minimum(tallies[giver] - 1, bound - tallies[sink]) // 2
    room = jnp.where((giver == order[0]) | (sink == order[0]) | (tallies[sink] == 0), 0, jnp.maximum(room, 0))
    passed = jax.random.randint(jax.random.fold_in(own, 4), (count // 2,), 0, 1 << 20) % (room + 1)
    tallies = tallies.at[giver].add(-passed).at[sink].add(passed)
    members = jnp.searchsorted(jnp.cumsum(tallies), jnp.arange(rows * top), side="right").astype(jnp.int32)
    table = members.reshape(top, rows).T
    table = table[jax.random.permutation(jax.random.fold_in(own, 1), rows)]
    offset_by = jax.random.randint(jax.random.fold_in(own, 2), (rows, 1), 0, top)
    return jnp.take_along_axis(table, (jnp.arange(top)[None, :] + offset_by) % top, axis=1)


def shares(number_of, total, reach, slope, full):
    loads = [(1 << 20) // math.isqrt(standing ** slope) + 1 for standing in range(1, number_of + 1)]
    largest = reach if full else min(reach, max(-(-total // number_of), total * loads[0] // sum(loads)))
    least = 1 if total - largest >= number_of - 1 else 0
    given, spare = [largest] + [least] * (number_of - 1), total - largest - least * (number_of - 1)
    while spare > 0:
        movable = [i for i in range(1, number_of) if given[i] < largest] or [i for i in range(1, number_of) if given[i] < reach]
        pool, left = sum([loads[i] for i in movable]), spare
        for i in movable:
            addition = min(reach - given[i], max(1, left * loads[i] // pool), spare)
            given[i] = given[i] + addition
            spare = spare - addition
    return np.array(given)


def noise(own_key, extent, width, reach, pieces=(), kind=jnp.bfloat16):
    result = width * jax.random.normal(own_key, extent, jnp.float32)
    if pieces:
        result = result * block_levels(own_key, extent, pieces, -0.22, 0.18)
    return jnp.clip(result, -reach, reach).astype(kind)


def heavy_noise(own_key, shape, deviation, most, pieces, heavy, held_as=jnp.bfloat16):
    values = deviation * jax.random.normal(own_key, shape, jnp.float32)
    if pieces:
        values = values * block_levels(own_key, shape, pieces, -0.22, 0.18)
    return jnp.clip(with_spikes(values, jax.random.fold_in(own_key, 3), *heavy), -most, most).astype(held_as)


def setup_inputs(seed: int = 0) -> dict:
    splits = jax.random.split(jax.random.key(seed), 7)
    cell_rows = heavy_noise(splits[0], (MICRO, TOKENS_MB, D), 1.0, 24.0, ((1, 256),), (1, 2, 256, 6.0))
    cotangent = noise(splits[1], (MICRO, TOKENS_MB, D), 0.05, 0.75, ((1, 256),))
    cluster_ids_keys = jax.random.split(jax.random.fold_in(splits[2], 1), MICRO * TOKENS_MB // MB_ROWS)
    cluster_ids_turns = jax.random.permutation(jax.random.fold_in(splits[2], 3), MICRO * TOKENS_MB // MB_ROWS)
    cluster_ids = jax.vmap(lambda own, number: deal_out(jax.random.fold_in(splits[2], 2), own, number, MB_ROWS, CLUSTERS, 1, CAP, 2))(cluster_ids_keys, cluster_ids_turns).reshape((MICRO, TOKENS_MB, 1))
    enc_weight = noise(splits[3], (D, D), D ** -0.5, 0.1875)
    up_weight = noise(splits[4], (CLUSTERS, D, H), D ** -0.5, 0.1875, ((0, 32),))
    down_weight = noise(splits[5], (CLUSTERS, D, H), H ** -0.5, 0.125, ((0, 32),))
    return {"cell_rows": cell_rows, "cotangent": cotangent, "cluster_ids": cluster_ids, "enc_weight": enc_weight, "up_weight": up_weight, "down_weight": down_weight}


epsilon = 1e-06

def silu_pair(pre_value):
    gate_value = jax.nn.sigmoid(pre_value)
    return (pre_value * gate_value, gate_value * (1.0 + pre_value * (1.0 - gate_value)))

def encode(features, enc_weight):
    pre_enc = jnp.dot(features, enc_weight, preferred_element_type=jnp.float32)
    silu_enc, slope_enc = silu_pair(pre_enc)
    encoded = features.astype(jnp.float32) + silu_enc
    inverse = lax.rsqrt(lax.optimization_barrier(jnp.mean(encoded * encoded, axis=-1, keepdims=True)) + epsilon)
    return (encoded, inverse, slope_enc)

def expert_pass(operands):
    norm_rows, grad_rows, w_up, w_down = operands
    norm_f32 = norm_rows.astype(jnp.float32)
    grad_f32 = grad_rows.astype(jnp.float32)
    up_f32 = w_up.astype(jnp.float32)
    pre_exp = jnp.einsum('drk,kh->drh', norm_f32, up_f32)
    silu_exp, slope_exp = silu_pair(pre_exp)
    active = silu_exp.astype(jnp.bfloat16)
    down_part = jnp.einsum('drk,drh->dkh', grad_f32, active.astype(jnp.float32)).astype(jnp.bfloat16)
    act_grad = jnp.einsum('drk,kh->drh', grad_f32, w_down.astype(jnp.float32))
    pre_grad = (act_grad * slope_exp).astype(jnp.bfloat16)
    up_part = jnp.einsum('drk,drh->dkh', norm_f32, pre_grad.astype(jnp.float32)).astype(jnp.bfloat16)
    back_rows = jnp.einsum('drh,kh->drk', pre_grad.astype(jnp.float32), up_f32).astype(jnp.bfloat16)
    up_sum = lax.optimization_barrier(jnp.sum(up_part.astype(jnp.float32), axis=0)).astype(jnp.bfloat16)
    down_sum = lax.optimization_barrier(jnp.sum(down_part.astype(jnp.float32), axis=0)).astype(jnp.bfloat16)
    return (up_sum, down_sum, back_rows)

def reference(cell_rows, cotangent, cluster_ids, enc_weight, up_weight, down_weight):
    devices_all = N_DP * N_EXPERT
    labels = cluster_ids[..., 0].astype(jnp.int32)
    blocks = labels.reshape(MICRO, devices_all, MB_ROWS)
    onehot = (blocks[..., None] == jnp.arange(CLUSTERS, dtype=jnp.int32)).astype(jnp.int32)
    before = (jnp.cumsum(onehot, axis=2) - onehot).astype(jnp.int32)
    slot_rank = lax.optimization_barrier(jnp.sum(before * onehot, axis=-1)).astype(jnp.int32)
    source = jnp.arange(devices_all, dtype=jnp.int32)
    dp_of = source // N_EXPERT
    ex_of = source % N_EXPERT
    per_batch = N_EXPERT * CAP
    bucket_rows = MICRO * per_batch
    batch_of = jnp.arange(MICRO, dtype=jnp.int32)
    target = ((blocks * N_DP + dp_of[None, :, None]) * bucket_rows + batch_of[:, None, None] * per_batch + ex_of[None, :, None] * CAP + slot_rank).reshape(-1).astype(jnp.int32)
    normed_list = []
    for batch_index in range(MICRO):
        encoded, inverse, slope_enc = encode(cell_rows[batch_index], enc_weight)
        normed_list.append((encoded * inverse).astype(jnp.bfloat16))
    normed_all = jnp.stack(normed_list).reshape(-1, D)
    slot_total = CLUSTERS * N_DP * bucket_rows
    sent_norm = jnp.zeros((slot_total, D), jnp.bfloat16).at[target].set(normed_all)
    sent_grad = jnp.zeros((slot_total, D), jnp.bfloat16).at[target].set(cotangent.reshape(-1, D))
    sent_norm = sent_norm.reshape(CLUSTERS, N_DP, bucket_rows, D)
    sent_grad = sent_grad.reshape(CLUSTERS, N_DP, bucket_rows, D)
    up_grad, down_grad, returned = lax.map(expert_pass, (sent_norm, sent_grad, up_weight, down_weight))
    norm_back = returned.reshape(slot_total, D)[target].reshape(MICRO, TOKENS_MB, D)
    enc_grad = jnp.zeros((D, D), jnp.float32)
    for batch_index in range(MICRO):
        encoded, inverse, slope_enc = encode(cell_rows[batch_index], enc_weight)
        norm_grad = norm_back[batch_index].astype(jnp.float32)
        enc_rows_grad = inverse * norm_grad - inverse * inverse * inverse * encoded * lax.optimization_barrier(jnp.mean(norm_grad * encoded, axis=-1, keepdims=True))
        enc_pre_grad = (enc_rows_grad * slope_enc).astype(jnp.bfloat16)
        enc_grad = enc_grad + jnp.dot(cell_rows[batch_index].T, enc_pre_grad, preferred_element_type=jnp.float32)
    return (enc_grad, up_grad, down_grad)
```

```python
import jax
import jax.numpy as jnp
from jax import lax
from jax.sharding import PartitionSpec as P

epsilon = 1e-06
contract_rows = (((0,), (0,)), ((), ()))


def silu_pair(pre_value):
    gate_value = jax.nn.sigmoid(pre_value)
    return (pre_value * gate_value, gate_value * (1.0 + pre_value * (1.0 - gate_value)))


def body(cell_rows, cotangent, cluster_ids, enc_weight, up_weight, down_weight):
    experts = lax.axis_size("expert")
    dp_count = lax.axis_size("dp")
    batch_count, local_rows, width = cell_rows.shape
    capacity = 8
    w_up = up_weight[0]
    w_down = down_weight[0]
    rows = batch_count * local_rows
    slots = experts * batch_count * capacity
    features = cell_rows.reshape(rows, width)
    pre_enc = jnp.dot(features, enc_weight, preferred_element_type=jnp.float32)
    silu_enc, slope_enc = silu_pair(pre_enc)
    encoded = features.astype(jnp.float32) + silu_enc
    inverse = lax.rsqrt(jnp.mean(encoded * encoded, axis=1, keepdims=True) + epsilon)
    normed = (encoded * inverse).astype(jnp.bfloat16)
    labels = cluster_ids[:, :, 0]
    onehot = (labels[:, :, None] == jnp.arange(experts, dtype=jnp.int32)).astype(jnp.int32)
    rank = jnp.sum((jnp.cumsum(onehot, axis=1) - onehot) * onehot, axis=2)
    batch_of = jnp.arange(batch_count, dtype=jnp.int32)[:, None]
    target = ((labels * batch_count + batch_of) * capacity + rank).reshape(rows)
    placer = (jnp.arange(slots, dtype=jnp.int32)[:, None] == target[None, :]).astype(jnp.bfloat16)
    both = jnp.concatenate([normed, cotangent.reshape(rows, width)], axis=1)
    send = jnp.dot(placer, both, preferred_element_type=jnp.float32).astype(jnp.bfloat16)
    recv = lax.all_to_all(
        send.reshape(experts, batch_count * capacity, 2 * width), "expert", split_axis=0, concat_axis=0, tiled=True
    ).reshape(slots, 2 * width)
    norm_rows, grad_rows = recv[:, :width], recv[:, width:]
    pre_exp = jnp.dot(norm_rows, w_up, preferred_element_type=jnp.float32)
    silu_exp, slope_exp = silu_pair(pre_exp)
    active = silu_exp.astype(jnp.bfloat16)
    act_grad = jnp.dot(grad_rows, w_down, preferred_element_type=jnp.float32)
    pre_grad = (act_grad * slope_exp).astype(jnp.bfloat16)
    up_part = lax.dot_general(norm_rows, pre_grad, contract_rows, preferred_element_type=jnp.float32).astype(jnp.bfloat16)
    down_part = lax.dot_general(grad_rows, active, contract_rows, preferred_element_type=jnp.float32).astype(jnp.bfloat16)
    up_sum = lax.psum_scatter(up_part, "dp", scatter_dimension=0, tiled=True)
    down_sum = lax.psum_scatter(down_part, "dp", scatter_dimension=0, tiled=True)
    back_rows = lax.dot_general(
        pre_grad, w_up, (((1,), (1,)), ((), ())), preferred_element_type=jnp.float32
    ).astype(jnp.bfloat16)
    returned = lax.all_to_all(
        back_rows.reshape(experts, batch_count * capacity, width), "expert", split_axis=0, concat_axis=0, tiled=True
    ).reshape(slots, width)
    norm_grad = lax.dot_general(placer, returned, contract_rows, preferred_element_type=jnp.float32)
    enc_rows_grad = inverse * norm_grad - inverse * inverse * inverse * encoded * jnp.mean(
        norm_grad * encoded, axis=1, keepdims=True
    )
    enc_pre_grad = (enc_rows_grad * slope_enc).astype(jnp.bfloat16)
    enc_part = lax.dot_general(features, enc_pre_grad, contract_rows, preferred_element_type=jnp.float32)
    enc_dp = lax.psum_scatter(enc_part, "dp", scatter_dimension=0, tiled=True)
    enc_sum = lax.psum_scatter(enc_dp, "expert", scatter_dimension=0, tiled=True)
    return (enc_sum, up_sum[None], down_sum[None])


def solution(mesh):
    in_specs = (
        P(None, ("dp", "expert"), None),
        P(None, ("dp", "expert"), None),
        P(None, ("dp", "expert"), None),
        P(),
        P("expert", None, None),
        P("expert", None, None),
    )
    out_specs = (P(("dp", "expert"), None), P("expert", "dp", None), P("expert", "dp", None))
    return jax.shard_map(body, mesh=mesh, in_specs=in_specs, out_specs=out_specs, check_vma=False)
```

```python
import jax
import jax.numpy as jnp
from jax import lax
from jax.experimental import pallas as pl
from jax.experimental.pallas import tpu as pltpu
from jax.sharding import PartitionSpec as P

MESH = pl.DeviceIdType.MESH
F32 = jnp.float32
BF16 = jnp.bfloat16
epsilon = 1e-06

N_DP = 8
N_EX = 32
D = 1024
H = 2048
ROWS = 128
MICRO = 2
ALL_ROWS = MICRO * ROWS
CAP = 8
SLOT = MICRO * CAP
SLOTS = N_EX * SLOT
WIDE = 512


def dot(a, b):
    return jnp.dot(a, b, preferred_element_type=F32)


def dot_nt(a, b):
    return lax.dot_general(a, b, (((1,), (1,)), ((), ())), preferred_element_type=F32)


def dot_tn(a, b):
    return lax.dot_general(a, b, (((0,), (0,)), ((), ())), preferred_element_type=F32)


def aligned(index, size):
    return pl.ds(pl.multiple_of(index * size, size), size)


def loop(low, high, step):
    def body(index, carry):
        step(index)
        return carry

    lax.fori_loop(low, high, body, 0)


def kernel(
    cell, cot, ids, encw, up_hbm, down_hbm,
    enc_out, up_out, down_out,
    w_up, w_down, both, send, recv, pre_grad, active, back, ret,
    enc_s, slope_s, inv_s, placer, fperm, egrad,
    part, rs_recv, z_recv,
    e_own, e_send, e_recv, x_own, x_send, x_recv, h_own, h_send, h_recv, d_send, d_recv,
    w_sem, disp_s, disp_r, ret_s, ret_r, rs_s, rs_r, z_s, z_r, c_s, c_r, x_s, x_r, h_s, h_r, d_s, d_r,
):
    d = lax.axis_index("dp")
    e = lax.axis_index("expert")
    z_lo, y = d // 4, d % 4
    z_hi, plane = e // 8, e % 8
    x, core = plane // 2, plane % 2
    right = (z_lo * 4 + (y + 1) % 4, e)
    left = (z_lo * 4 + (y + 3) % 4, e)
    mate = ((1 - z_lo) * 4 + y, e)

    def copy(src, dst, s, r, who):
        return pltpu.make_async_remote_copy(
            src_ref=src, dst_ref=dst, send_sem=s, recv_sem=r, device_id=who, device_id_type=MESH
        )

    w_copies = [
        pltpu.make_async_copy(up_hbm.at[0], w_up, w_sem.at[0]),
        pltpu.make_async_copy(down_hbm.at[0], w_down, w_sem.at[1]),
    ]
    for item in w_copies:
        item.start()

    barrier = pltpu.get_barrier_semaphore()

    def greet_expert(k):
        pl.semaphore_signal(barrier, inc=1, device_id=(d, (e + k) % N_EX), device_id_type=MESH)

    def greet_dp(k):
        pl.semaphore_signal(barrier, inc=1, device_id=((d + k) % N_DP, e), device_id_type=MESH)

    loop(1, N_EX, greet_expert)
    loop(1, N_DP, greet_dp)

    lower = (
        lax.broadcasted_iota(jnp.int32, (ROWS, ROWS), 1) < lax.broadcasted_iota(jnp.int32, (ROWS, ROWS), 0)
    ).astype(BF16)
    for m in range(MICRO):
        label = ids[m]
        onehot = (label == lax.broadcasted_iota(jnp.int32, (ROWS, 128), 1)).astype(F32)
        before = dot(lower, onehot.astype(BF16))
        rank = jnp.sum(before * onehot, axis=1, keepdims=True).astype(jnp.int32)
        target = label * SLOT + m * CAP + rank
        slots = lax.broadcasted_iota(jnp.int32, (ROWS, SLOTS), 1)
        placer[m * ROWS : (m + 1) * ROWS, :] = (slots == target).astype(F32).astype(BF16)

    def encode(i):
        m, part_row = i // 2, i % 2
        rows = aligned(part_row, 64)
        feat = cell[m, rows, :]
        pre = dot(feat, encw[...])
        gate = jax.nn.sigmoid(pre)
        encoded = feat.astype(F32) + pre * gate
        inverse = lax.rsqrt(jnp.sum(encoded * encoded, axis=1, keepdims=True) * (1.0 / D) + epsilon)
        out = aligned(i, 64)
        enc_s[out, :] = encoded
        slope_s[out, :] = gate * (1.0 + pre * (1.0 - gate))
        inv_s[out, :] = jnp.broadcast_to(inverse, (64, 128))
        both[out, :D] = (encoded * inverse).astype(BF16)
        both[out, D:] = cot[m, rows, :]

    loop(0, 4, encode)
    pl.semaphore_wait(barrier, N_EX + N_DP - 2)

    def dispatch(c):
        return copy(send.at[aligned(c, SLOT), :], recv.at[aligned(e, SLOT), :], disp_s.at[c], disp_r.at[e], (d, c))

    def arrival(c):
        return copy(send.at[aligned(c, SLOT), :], recv.at[aligned(c, SLOT), :], disp_s.at[c], disp_r.at[c], (d, c))

    order = (0, 1, 3, 2)

    def peer(hop, k):
        return ((z_hi + hop) % 4) * 8 + (plane + k) % 8

    for hop in order:
        h = (z_hi + hop) % 4
        picks = placer[:, aligned(h, 128)]
        send[aligned(h, 128), :] = dot_tn(picks, both[...]).astype(BF16)
        loop(1 if hop == 0 else 0, 8, lambda k: dispatch(peer(hop, k)).start())
    recv[aligned(e, SLOT), :] = send[aligned(e, SLOT), :]

    def permute(n):
        col = lax.broadcasted_iota(jnp.int32, (1, 256), 1) + n * 256
        nat = (
            (col & 3)
            + (((col >> 2) & 7) << 7)
            + (((col >> 5) & 3) << 5)
            + (((col >> 7) & 3) << 3)
            + ((col >> 9) << 2)
        )
        pick = (lax.broadcasted_iota(jnp.int32, (D, 256), 0) == nat).astype(F32).astype(BF16)
        for m in range(MICRO):
            fperm[m * ROWS : (m + 1) * ROWS, aligned(n, 256)] = dot(cell[m], pick).astype(BF16)

    loop(0, 4, permute)
    for item in w_copies:
        item.wait()

    def give_back(c):
        return copy(back.at[aligned(c, SLOT), :], ret.at[aligned(e, SLOT), :], ret_s.at[c], ret_r.at[e], (d, c))

    def came_back(c):
        return copy(back.at[aligned(c, SLOT), :], ret.at[aligned(c, SLOT), :], ret_s.at[c], ret_r.at[c], (d, c))

    for hop in order:
        h = (z_hi + hop) % 4
        group = aligned(h, 128)
        loop(1 if hop == 0 else 0, 8, lambda k: arrival(peer(hop, k)).wait_recv())

        def hidden(n):
            cols = aligned(n, WIDE)
            pre = dot(recv[group, :D], w_up[:, cols])
            act_grad = dot(recv[group, D:], w_down[:, cols])
            gate = jax.nn.sigmoid(pre)
            active[group, cols] = (pre * gate).astype(BF16)
            pre_grad[group, cols] = (act_grad * (gate * (1.0 + pre * (1.0 - gate)))).astype(BF16)

        loop(0, H // WIDE, hidden)

        def backward(n):
            back[group, aligned(n, 256)] = dot_nt(pre_grad[group, :], w_up[aligned(n, 256), :]).astype(BF16)

        loop(0, D // 256, backward)
        if hop == 0:
            loop(1, 8, lambda k: give_back(peer(0, k)).start())
    for hop in order[1:]:
        loop(0, 8, lambda k: give_back(peer(hop, k)).start())
    ret[aligned(e, SLOT), :] = back[aligned(e, SLOT), :]

    def grads(p, q, block):
        up_t = recv[:, aligned(block, 128)].T
        down_t = recv[:, aligned(block + D // 128, 128)].T

        def piece(n):
            cols = aligned(n, WIDE)
            part[p, q, 0, :, cols] = dot(up_t, pre_grad[:, cols]).astype(BF16)
            part[p, q, 1, :, cols] = dot(down_t, active[:, cols]).astype(BF16)

        loop(0, H // WIDE, piece)

    def rs(p, slot):
        q, which, who = ((0, 0, right), (0, 1, left), (1, 1, right), (2, 0, left), (1, 0, right), (2, 1, left))[slot]
        return copy(part.at[p, q, which], rs_recv.at[p, slot], rs_s.at[p, slot], rs_r.at[p, slot], who)

    def add_into(p, q, which, others):
        def piece(n):
            rows = aligned(n, 32)
            total = part[p, q, which, rows, :].astype(F32)
            for slot in others:
                total = total + rs_recv[p, slot, rows, :].astype(F32)
            part[p, q, which, rows, :] = total.astype(BF16)

        loop(0, 4, piece)

    for p in range(2):
        base = ((1 - z_lo) if p == 0 else z_lo) * 4
        grads(p, 0, base + (y + 2) % 4)
        rs(p, 0).start()
        rs(p, 1).start()
        if p == 0:
            grads(p, 1, base + (y + 1) % 4)
            rs(p, 2).start()
            grads(p, 2, base + (y + 3) % 4)
            rs(p, 3).start()
            grads(p, 3, base + y)

    def combine(p):
        rs(p, 0).wait_recv()
        add_into(p, 1, 0, (0,))
        rs(p, 4).start()
        rs(p, 1).wait_recv()
        add_into(p, 2, 1, (1,))
        rs(p, 5).start()

    combine(0)
    base = z_lo * 4
    grads(1, 1, base + (y + 1) % 4)
    rs(1, 2).start()
    grads(1, 2, base + (y + 3) % 4)
    rs(1, 3).start()
    grads(1, 3, base + y)

    loop(1, 8, lambda k: came_back(peer(0, k)).wait_recv())
    for hop in order[1:]:
        loop(0, 8, lambda k: came_back(peer(hop, k)).wait_recv())

    def encoder_back(i):
        rows = aligned(i, 64)
        norm_grad = dot(placer[rows, :], ret[...])
        encoded = enc_s[rows, :]
        inverse = inv_s[rows, 0:1]
        mean = jnp.sum(norm_grad * encoded, axis=1, keepdims=True) * (1.0 / D)
        grad = inverse * norm_grad - inverse * inverse * inverse * encoded * mean
        egrad[rows, :] = (grad * slope_s[rows, :]).astype(BF16)

    loop(0, 4, encoder_back)

    def enc_piece(index):
        return dot(fperm[:, aligned(index, 128)].T, egrad[...])

    def enc_other(n):
        e_send[aligned(n, 128), :] = enc_piece((1 - core) * 4 + n).astype(BF16)

    def enc_own(n):
        e_own[aligned(n, 128), :] = enc_piece(core * 4 + n)

    loop(0, 4, enc_other)
    to_core = copy(e_send, e_recv, c_s.at[0], c_r.at[0], (d, e + 1 - 2 * core))
    to_core.start()
    loop(0, 4, enc_own)

    combine(1)

    to_core.wait_recv()

    def x_device(k):
        return (x + k) % 4

    def x_copy(k):
        to = x_device(k)
        return copy(x_send.at[to], x_recv.at[x], x_s.at[to], x_r.at[x], (d, (z_hi * 4 + to) * 2 + core))

    def x_from(k):
        to = x_device(k)
        return copy(x_send.at[to], x_recv.at[to], x_s.at[to], x_r.at[to], (d, (z_hi * 4 + to) * 2 + core))

    for k in (2, 1, 3):
        rows = aligned(x_device(k), 128)
        x_send[x_device(k)] = (e_own[rows, :] + e_recv[rows, :].astype(F32)).astype(BF16)
        x_copy(k).start()
    rows = aligned(x, 128)
    x_own[...] = e_own[rows, :] + e_recv[rows, :].astype(F32)

    def finish(p):
        rs(p, 3).wait_recv()
        rs(p, 4).wait_recv()
        rs(p, 2).wait_recv()
        rs(p, 5).wait_recv()

    finish(0)
    to_mate = [copy(part.at[0, 3, w], z_recv.at[w], z_s.at[w], z_r.at[w], mate) for w in range(2)]
    add_into(0, 3, 0, (3, 4))
    to_mate[0].start()
    add_into(0, 3, 1, (2, 5))
    to_mate[1].start()

    for k in (1, 3, 2):
        x_from(k).wait_recv()

    def h_copy(k):
        to = (z_hi + k) % 4
        return copy(h_send.at[to], h_recv.at[z_hi], h_s.at[to], h_r.at[z_hi], (d, to * 8 + plane))

    def h_from(k):
        to = (z_hi + k) % 4
        return copy(h_send.at[to], h_recv.at[to], h_s.at[to], h_r.at[to], (d, to * 8 + plane))

    def x_sum(to):
        rows = aligned(to, 32)
        total = x_own[rows, :]
        for k in (1, 2, 3):
            total = total + x_recv[x_device(k), rows, :].astype(F32)
        return total

    for k in (2, 1, 3):
        h_send[(z_hi + k) % 4] = x_sum((z_hi + k) % 4).astype(BF16)
        h_copy(k).start()
    h_own[...] = x_sum(z_hi)
    for k in (1, 3, 2):
        h_from(k).wait_recv()
    total = h_own[...]
    for k in (1, 2, 3):
        total = total + h_recv[(z_hi + k) % 4].astype(F32)
    d_send[...] = total.reshape(N_DP, 4, D)

    def d_copy(k):
        to = (d + k) % N_DP
        return copy(d_send.at[to], d_recv.at[d], d_s.at[to], d_r.at[d], (to, e))

    def d_from(k):
        to = (d + k) % N_DP
        return copy(d_send.at[to], d_recv.at[to], d_s.at[to], d_r.at[to], (to, e))

    loop(1, N_DP, lambda k: d_copy(k).start())

    finish(1)
    for w, (out, others) in enumerate(((up_out, (3, 4)), (down_out, (2, 5)))):
        to_mate[w].wait_recv()

        def piece(n):
            rows = aligned(n, 32)
            total = part[1, 3, w, rows, :].astype(F32) + z_recv[w, rows, :].astype(F32)
            for slot in others:
                total = total + rs_recv[1, slot, rows, :].astype(F32)
            out[0, rows, :] = total.astype(BF16)

        loop(0, 4, piece)

    loop(1, N_DP, lambda k: d_from(k).wait_recv())
    total = d_send[d]
    for k in range(1, N_DP):
        total = total + d_recv[(d + k) % N_DP]
    enc_out[...] = total

    for hop in order:
        loop(1 if hop == 0 else 0, 8, lambda k: dispatch(peer(hop, k)).wait_send())
        loop(1 if hop == 0 else 0, 8, lambda k: give_back(peer(hop, k)).wait_send())
    for p in range(2):
        for slot in range(6):
            rs(p, slot).wait_send()
    for w in range(2):
        to_mate[w].wait_send()
    to_core.wait_send()
    for k in (1, 2, 3):
        x_copy(k).wait_send()
        h_copy(k).wait_send()
    loop(1, N_DP, lambda k: d_copy(k).wait_send())


def body(cell_rows, cotangent, cluster_ids, enc_weight, up_weight, down_weight):
    vmem = pl.BlockSpec(memory_space=pltpu.VMEM)
    hbm = pl.BlockSpec(memory_space=pl.ANY)
    dma = pltpu.SemaphoreType.DMA
    return pl.pallas_call(
        kernel,
        name="step",
        out_shape=(
            jax.ShapeDtypeStruct((4, D), F32),
            jax.ShapeDtypeStruct((1, 128, H), BF16),
            jax.ShapeDtypeStruct((1, 128, H), BF16),
        ),
        in_specs=[vmem, vmem, vmem, vmem, hbm, hbm],
        out_specs=(vmem, vmem, vmem),
        scratch_shapes=[
            pltpu.VMEM((D, H), BF16),
            pltpu.VMEM((D, H), BF16),
            pltpu.VMEM((ALL_ROWS, 2 * D), BF16),
            pltpu.VMEM((SLOTS, 2 * D), BF16),
            pltpu.VMEM((SLOTS, 2 * D), BF16),
            pltpu.VMEM((SLOTS, H), BF16),
            pltpu.VMEM((SLOTS, H), BF16),
            pltpu.VMEM((SLOTS, D), BF16),
            pltpu.VMEM((SLOTS, D), BF16),
            pltpu.VMEM((ALL_ROWS, D), F32),
            pltpu.VMEM((ALL_ROWS, D), F32),
            pltpu.VMEM((ALL_ROWS, 128), F32),
            pltpu.VMEM((ALL_ROWS, SLOTS), BF16),
            pltpu.VMEM((ALL_ROWS, D), BF16),
            pltpu.VMEM((ALL_ROWS, D), BF16),
            pltpu.VMEM((2, 4, 2, 128, H), BF16),
            pltpu.VMEM((2, 6, 128, H), BF16),
            pltpu.VMEM((2, 128, H), BF16),
            pltpu.VMEM((512, D), F32),
            pltpu.VMEM((512, D), BF16),
            pltpu.VMEM((512, D), BF16),
            pltpu.VMEM((128, D), F32),
            pltpu.VMEM((4, 128, D), BF16),
            pltpu.VMEM((4, 128, D), BF16),
            pltpu.VMEM((32, D), F32),
            pltpu.VMEM((4, 32, D), BF16),
            pltpu.VMEM((4, 32, D), BF16),
            pltpu.VMEM((N_DP, 4, D), F32),
            pltpu.VMEM((N_DP, 4, D), F32),
            dma((2,)),
            dma((N_EX,)),
            dma((N_EX,)),
            dma((N_EX,)),
            dma((N_EX,)),
            dma((2, 6)),
            dma((2, 6)),
            dma((2,)),
            dma((2,)),
            dma((1,)),
            dma((1,)),
            dma((4,)),
            dma((4,)),
            dma((4,)),
            dma((4,)),
            dma((N_DP,)),
            dma((N_DP,)),
        ],
        compiler_params=pltpu.CompilerParams(
            collective_id=0, has_side_effects=True, vmem_limit_bytes=62 << 20
        ),
    )(cell_rows, cotangent, cluster_ids, enc_weight, up_weight, down_weight)


def solution(mesh):
    in_specs = (
        P(None, ("dp", "expert"), None),
        P(None, ("dp", "expert"), None),
        P(None, ("dp", "expert"), None),
        P(),
        P("expert", None, None),
        P("expert", None, None),
    )
    out_specs = (P(("dp", "expert"), None), P("expert", "dp", None), P("expert", "dp", None))
    return jax.shard_map(body, mesh=mesh, in_specs=in_specs, out_specs=out_specs, check_vma=False)
```

```python
import jax
import jax.numpy as jnp
from jax import lax
from jax.experimental import pallas as pl
from jax.experimental.pallas import tpu as pltpu
from jax.sharding import PartitionSpec as P

MESH = pl.DeviceIdType.MESH
F32 = jnp.float32
BF16 = jnp.bfloat16
epsilon = 1e-06

N_DP = 8
N_EX = 32
D = 1024
H = 2048
ROWS = 128
MICRO = 2
ALL_ROWS = MICRO * ROWS
CAP = 8
SLOT = MICRO * CAP
SLOTS = N_EX * SLOT
WIDE = 512
EARLY = 512


def dot(a, b):
    return jnp.dot(a, b, preferred_element_type=F32)


def dot_nt(a, b):
    return lax.dot_general(a, b, (((1,), (1,)), ((), ())), preferred_element_type=F32)


def dot_tn(a, b):
    return lax.dot_general(a, b, (((0,), (0,)), ((), ())), preferred_element_type=F32)


def aligned(index, size):
    return pl.ds(pl.multiple_of(index * size, size), size)


def loop(low, high, step):
    def body(index, carry):
        step(index)
        return carry

    lax.fori_loop(low, high, body, 0)


def kernel(
    cell, cot, ids, encw_hbm, up_hbm, down_hbm,
    enc_out, up_out, down_out,
    encw, w_up, w_down, normed, send_n, send_g, recv_n, recv_g, pre_grad, active, back, ret,
    enc_s, slope_s, inv_s, placer, fperm, egrad,
    part, rs_recv, z_recv, early_recv,
    e_own, e_send, e_recv, x_own, x_send, x_recv, h_own, h_send, h_recv, d_send, d_recv,
    w_sem, disp_s, disp_r, dispg_s, dispg_r, early_s, early_r, ret_s, ret_r, rs_s, rs_r, z_s, z_r, c_s, c_r, x_s, x_r, h_s, h_r, d_s, d_r,
):
    d = lax.axis_index("dp")
    e = lax.axis_index("expert")
    z_lo, y = d // 4, d % 4
    z_hi, plane = e // 8, e % 8
    x, core = plane // 2, plane % 2
    right = (z_lo * 4 + (y + 1) % 4, e)
    left = (z_lo * 4 + (y + 3) % 4, e)
    mate = ((1 - z_lo) * 4 + y, e)

    def copy(src, dst, s, r, who):
        return pltpu.make_async_remote_copy(
            src_ref=src, dst_ref=dst, send_sem=s, recv_sem=r, device_id=who, device_id_type=MESH
        )

    enc_copy = pltpu.make_async_copy(encw_hbm, encw, w_sem.at[2])
    enc_copy.start()
    w_copies = [
        pltpu.make_async_copy(up_hbm.at[0], w_up, w_sem.at[0]),
        pltpu.make_async_copy(down_hbm.at[0], w_down, w_sem.at[1]),
    ]
    for item in w_copies:
        item.start()

    barrier = pltpu.get_barrier_semaphore()

    def greet_expert(k):
        pl.semaphore_signal(barrier, inc=1, device_id=(d, (e + k) % N_EX), device_id_type=MESH)

    def greet_dp(k):
        pl.semaphore_signal(barrier, inc=1, device_id=((d + k) % N_DP, e), device_id_type=MESH)

    loop(1, N_EX, greet_expert)
    loop(1, N_DP, greet_dp)

    upper = (
        lax.broadcasted_iota(jnp.int32, (ROWS, ROWS), 0) < lax.broadcasted_iota(jnp.int32, (ROWS, ROWS), 1)
    ).astype(F32).astype(BF16)
    for m in range(MICRO):
        label = ids[m : m + 1, :]
        onehot = (label == lax.broadcasted_iota(jnp.int32, (N_EX, ROWS), 0)).astype(F32)
        before = dot(onehot.astype(BF16), upper)
        rank = jnp.sum(before * onehot, axis=0, keepdims=True).astype(jnp.int32)
        target = label * SLOT + m * CAP + rank
        slots = lax.broadcasted_iota(jnp.int32, (SLOTS, ROWS), 0)
        placer[:, m * ROWS : (m + 1) * ROWS] = (slots == target).astype(F32).astype(BF16)

    def to_g(c):
        return copy(send_g.at[aligned(c, SLOT), :], recv_g.at[aligned(e, SLOT), :], dispg_s.at[c], dispg_r.at[e], (d, c))

    def from_g(c):
        return copy(send_g.at[aligned(c, SLOT), :], recv_g.at[aligned(c, SLOT), :], dispg_s.at[c], dispg_r.at[c], (d, c))

    def to_n(c):
        return copy(send_n.at[aligned(c, SLOT), :], recv_n.at[aligned(e, SLOT), :], disp_s.at[c], disp_r.at[e], (d, c))

    def from_n(c):
        return copy(send_n.at[aligned(c, SLOT), :], recv_n.at[aligned(c, SLOT), :], disp_s.at[c], disp_r.at[c], (d, c))

    order = (0, 1, 3, 2)
    far_first = (1, 3, 2, 0)

    def peer(hop, k):
        return ((z_hi + hop) % 4) * 8 + (plane + k) % 8

    def peers(hop, step):
        loop(1 if hop == 0 else 0, 8, lambda k: step(peer(hop, k)))

    for hop in far_first:
        group = aligned((z_hi + hop) % 4, 128)
        send_g[group, :] = dot(placer[group, :], cot[...]).astype(BF16)
        if hop == far_first[0]:
            pl.semaphore_wait(barrier, N_EX + N_DP - 2)
        peers(hop, lambda c: to_g(c).start())
    recv_g[aligned(e, SLOT), :] = send_g[aligned(e, SLOT), :]

    inv_s[...] = jnp.zeros_like(inv_s)
    enc_copy.wait()

    def encode(n):
        cols = aligned(n, 256)
        pre = dot(cell[...], encw[:, cols])
        gate = jax.nn.sigmoid(pre)
        encoded = cell[:, cols].astype(F32) + pre * gate
        enc_s[:, cols] = encoded
        slope_s[:, cols] = gate * (1.0 + pre * (1.0 - gate))
        square = encoded * encoded
        inv_s[...] += square[:, :128] + square[:, 128:]

    loop(0, 4, encode)

    def normalize(i):
        rows = aligned(i, 64)
        inverse = lax.rsqrt(jnp.sum(inv_s[rows, :], axis=1, keepdims=True) * (1.0 / D) + epsilon)
        inv_s[rows, :] = jnp.broadcast_to(inverse, (64, 128))
        normed[rows, :] = (enc_s[rows, :] * inverse).astype(BF16)

    loop(0, 4, normalize)
    for hop in far_first:
        group = aligned((z_hi + hop) % 4, 128)
        send_n[group, :] = dot(placer[group, :], normed[...]).astype(BF16)
        peers(hop, lambda c: to_n(c).start())
    recv_n[aligned(e, SLOT), :] = send_n[aligned(e, SLOT), :]

    def permute(n):
        col = lax.broadcasted_iota(jnp.int32, (1, 256), 1) + n * 256
        nat = (
            (col & 3)
            + (((col >> 2) & 7) << 7)
            + (((col >> 5) & 3) << 5)
            + (((col >> 7) & 3) << 3)
            + ((col >> 9) << 2)
        )
        pick = (lax.broadcasted_iota(jnp.int32, (D, 256), 0) == nat).astype(F32).astype(BF16)
        fperm[:, aligned(n, 256)] = dot(cell[...], pick).astype(BF16)

    loop(0, 4, permute)
    for item in w_copies:
        item.wait()

    def give_back(c):
        return copy(back.at[aligned(c, SLOT), :], ret.at[aligned(e, SLOT), :], ret_s.at[c], ret_r.at[e], (d, c))

    def came_back(c):
        return copy(back.at[aligned(c, SLOT), :], ret.at[aligned(c, SLOT), :], ret_s.at[c], ret_r.at[c], (d, c))

    def mlp(hop):
        group = aligned((z_hi + hop) % 4, 128)
        peers(hop, lambda c: from_g(c).wait_recv())
        peers(hop, lambda c: from_n(c).wait_recv())

        def hidden(n):
            cols = aligned(n, WIDE)
            pre = dot(recv_n[group, :], w_up[:, cols])
            act_grad = dot(recv_g[group, :], w_down[:, cols])
            gate = jax.nn.sigmoid(pre)
            active[group, cols] = (pre * gate).astype(BF16)
            pre_grad[group, cols] = (act_grad * (gate * (1.0 + pre * (1.0 - gate)))).astype(BF16)

        loop(0, H // WIDE, hidden)

    def mlp_back(hop):
        group = aligned((z_hi + hop) % 4, 128)

        def backward(n):
            back[group, aligned(n, 256)] = dot_nt(pre_grad[group, :], w_up[aligned(n, 256), :]).astype(BF16)

        loop(0, D // 256, backward)

    for hop in order:
        mlp(hop)
        if hop != order[-1]:
            mlp_back(hop)
        if hop == 0:
            peers(0, lambda c: give_back(c).start())

    def grads(p, q):
        block = ((1 - z_lo) if p == 0 else z_lo) * 4 + (y + (2, 1, 3, 0)[q]) % 4
        up_t = recv_n[:, aligned(block, 128)].T
        down_t = recv_g[:, aligned(block, 128)].T

        def piece(n):
            cols = aligned(n, WIDE)
            part[p, q, 0, :, cols] = dot(up_t, pre_grad[:, cols]).astype(BF16)
            part[p, q, 1, :, cols] = dot(down_t, active[:, cols]).astype(BF16)

        loop(0, H // WIDE, piece)

    late = (pl.ds(EARLY, H - EARLY), pl.ds(0, H))

    def rs(p, slot):
        q, which, who = ((0, 0, right), (0, 1, left), (1, 1, right), (2, 0, left), (1, 0, right), (2, 1, left))[slot]
        return copy(
            part.at[p, q, which, :, late[p]], rs_recv.at[p, slot, :, late[p]], rs_s.at[p, slot], rs_r.at[p, slot], who
        )

    def early(q, w):
        return copy(
            part.at[0, q, w, :, pl.ds(0, EARLY)], early_recv.at[q, w], early_s.at[q, w], early_r.at[q, w], mate
        )

    def add_early(q):
        for w in range(2):
            early(q, w).wait_recv()

            def piece(n):
                rows = aligned(n, 64)
                total = part[1, q, w, rows, :EARLY].astype(F32) + early_recv[q, w, rows, :].astype(F32)
                part[1, q, w, rows, :EARLY] = total.astype(BF16)

            loop(0, 2, piece)

    def add_into(p, q, which, others):
        def piece(n):
            rows = aligned(n, 32)
            total = part[p, q, which, rows, late[p]].astype(F32)
            for slot in others:
                total = total + rs_recv[p, slot, rows, late[p]].astype(F32)
            part[p, q, which, rows, late[p]] = total.astype(BF16)

        loop(0, 4, piece)

    def combine(p):
        rs(p, 0).wait_recv()
        add_into(p, 1, 0, (0,))
        rs(p, 4).start()
        rs(p, 1).wait_recv()
        add_into(p, 2, 1, (1,))
        rs(p, 5).start()

    grads(0, 0)
    rs(0, 0).start()
    rs(0, 1).start()
    early(0, 0).start()
    early(0, 1).start()
    mlp_back(order[-1])
    for hop in order[1:]:
        peers(hop, lambda c: give_back(c).start())
    ret[aligned(e, SLOT), :] = back[aligned(e, SLOT), :]
    for q in (1, 2, 3):
        grads(0, q)
        if q < 3:
            rs(0, q + 1).start()
        early(q, 0).start()
        early(q, 1).start()
    grads(1, 0)
    combine(0)
    for q in (1, 2, 3):
        grads(1, q)
    add_early(0)
    rs(1, 0).start()
    rs(1, 1).start()
    add_early(1)
    rs(1, 2).start()
    add_early(2)
    rs(1, 3).start()
    add_early(3)

    for hop in order:
        peers(hop, lambda c: came_back(c).wait_recv())

    def encoder_back(i):
        rows = aligned(i, 128)
        norm_grad = dot_tn(placer[:, rows], ret[...])
        encoded = enc_s[rows, :]
        inverse = inv_s[rows, 0:1]
        mean = jnp.sum(norm_grad * encoded, axis=1, keepdims=True) * (1.0 / D)
        grad = inverse * norm_grad - inverse * inverse * inverse * encoded * mean
        egrad[rows, :] = (grad * slope_s[rows, :]).astype(BF16)

    loop(0, 2, encoder_back)

    def enc_piece(index):
        return dot(fperm[:, aligned(index, 128)].T, egrad[...])

    def enc_other(n):
        e_send[aligned(n, 128), :] = enc_piece((1 - core) * 4 + n).astype(BF16)

    def enc_own(n):
        e_own[aligned(n, 128), :] = enc_piece(core * 4 + n)

    loop(0, 4, enc_other)
    to_core = copy(e_send, e_recv, c_s.at[0], c_r.at[0], (d, e + 1 - 2 * core))
    to_core.start()
    loop(0, 4, enc_own)

    combine(1)

    to_core.wait_recv()

    def x_device(k):
        return (x + k) % 4

    def x_copy(k):
        to = x_device(k)
        return copy(x_send.at[to], x_recv.at[x], x_s.at[to], x_r.at[x], (d, (z_hi * 4 + to) * 2 + core))

    def x_from(k):
        to = x_device(k)
        return copy(x_send.at[to], x_recv.at[to], x_s.at[to], x_r.at[to], (d, (z_hi * 4 + to) * 2 + core))

    for k in (2, 1, 3):
        rows = aligned(x_device(k), 128)
        x_send[x_device(k)] = (e_own[rows, :] + e_recv[rows, :].astype(F32)).astype(BF16)
        x_copy(k).start()
    rows = aligned(x, 128)
    x_own[...] = e_own[rows, :] + e_recv[rows, :].astype(F32)

    def finish(p):
        rs(p, 3).wait_recv()
        rs(p, 4).wait_recv()
        rs(p, 2).wait_recv()
        rs(p, 5).wait_recv()

    finish(0)
    to_mate = [
        copy(part.at[0, 3, w, :, late[0]], z_recv.at[w], z_s.at[w], z_r.at[w], mate) for w in range(2)
    ]
    add_into(0, 3, 0, (3, 4))
    to_mate[0].start()
    add_into(0, 3, 1, (2, 5))
    to_mate[1].start()

    for k in (1, 3, 2):
        x_from(k).wait_recv()

    def h_copy(k):
        to = (z_hi + k) % 4
        return copy(h_send.at[to], h_recv.at[z_hi], h_s.at[to], h_r.at[z_hi], (d, to * 8 + plane))

    def h_from(k):
        to = (z_hi + k) % 4
        return copy(h_send.at[to], h_recv.at[to], h_s.at[to], h_r.at[to], (d, to * 8 + plane))

    def x_sum(to):
        rows = aligned(to, 32)
        total = x_own[rows, :]
        for k in (1, 2, 3):
            total = total + x_recv[x_device(k), rows, :].astype(F32)
        return total

    for k in (2, 1, 3):
        h_send[(z_hi + k) % 4] = x_sum((z_hi + k) % 4).astype(BF16)
        h_copy(k).start()
    h_own[...] = x_sum(z_hi)
    for k in (1, 3, 2):
        h_from(k).wait_recv()
    total = h_own[...]
    for k in (1, 2, 3):
        total = total + h_recv[(z_hi + k) % 4].astype(F32)
    d_send[...] = total.reshape(N_DP, 4, D)

    def d_copy(k):
        to = (d + k) % N_DP
        return copy(d_send.at[to], d_recv.at[d], d_s.at[to], d_r.at[d], (to, e))

    def d_from(k):
        to = (d + k) % N_DP
        return copy(d_send.at[to], d_recv.at[to], d_s.at[to], d_r.at[to], (to, e))

    loop(1, N_DP, lambda k: d_copy(k).start())

    finish(1)
    for w, (out, others) in enumerate(((up_out, (3, 4)), (down_out, (2, 5)))):
        to_mate[w].wait_recv()

        def piece(n):
            rows = aligned(n, 32)
            total = part[1, 3, w, rows, :].astype(F32)
            for slot in others:
                total = total + rs_recv[1, slot, rows, :].astype(F32)
            out[0, rows, :EARLY] = total[:, :EARLY].astype(BF16)
            out[0, rows, EARLY:] = (total[:, EARLY:] + z_recv[w, rows, :].astype(F32)).astype(BF16)

        loop(0, 4, piece)

    loop(1, N_DP, lambda k: d_from(k).wait_recv())
    total = d_send[d]
    for k in range(1, N_DP):
        total = total + d_recv[(d + k) % N_DP]
    enc_out[...] = total

    for hop in order:
        peers(hop, lambda c: to_g(c).wait_send())
        peers(hop, lambda c: to_n(c).wait_send())
        peers(hop, lambda c: give_back(c).wait_send())
    for p in range(2):
        for slot in range(6):
            rs(p, slot).wait_send()
    for w in range(2):
        to_mate[w].wait_send()
        for q in range(4):
            early(q, w).wait_send()
    to_core.wait_send()
    for k in (1, 2, 3):
        x_copy(k).wait_send()
        h_copy(k).wait_send()
    loop(1, N_DP, lambda k: d_copy(k).wait_send())


def settle(enc_in, up_in, down_in, enc_out, up_out, down_out):
    enc_out[...] = enc_in[...]
    up_out[...] = up_in[...]
    down_out[...] = down_in[...]


def body(cell_rows, cotangent, cluster_ids, enc_weight, up_weight, down_weight):
    vmem = pl.BlockSpec(memory_space=pltpu.VMEM)
    hbm = pl.BlockSpec(memory_space=pl.ANY)
    dma = pltpu.SemaphoreType.DMA
    outs = pl.pallas_call(
        kernel,
        name="step",
        out_shape=(
            jax.ShapeDtypeStruct((4, D), F32),
            jax.ShapeDtypeStruct((1, 128, H), BF16),
            jax.ShapeDtypeStruct((1, 128, H), BF16),
        ),
        in_specs=[vmem, vmem, vmem, hbm, hbm, hbm],
        out_specs=(vmem, vmem, vmem),
        scratch_shapes=[
            pltpu.VMEM((D, D), BF16),
            pltpu.VMEM((D, H), BF16),
            pltpu.VMEM((D, H), BF16),
            pltpu.VMEM((ALL_ROWS, D), BF16),
            pltpu.VMEM((SLOTS, D), BF16),
            pltpu.VMEM((SLOTS, D), BF16),
            pltpu.VMEM((SLOTS, D), BF16),
            pltpu.VMEM((SLOTS, D), BF16),
            pltpu.VMEM((SLOTS, H), BF16),
            pltpu.VMEM((SLOTS, H), BF16),
            pltpu.VMEM((SLOTS, D), BF16),
            pltpu.VMEM((SLOTS, D), BF16),
            pltpu.VMEM((ALL_ROWS, D), F32),
            pltpu.VMEM((ALL_ROWS, D), F32),
            pltpu.VMEM((ALL_ROWS, 128), F32),
            pltpu.VMEM((SLOTS, ALL_ROWS), BF16),
            pltpu.VMEM((ALL_ROWS, D), BF16),
            pltpu.VMEM((ALL_ROWS, D), BF16),
            pltpu.VMEM((2, 4, 2, 128, H), BF16),
            pltpu.VMEM((2, 6, 128, H), BF16),
            pltpu.VMEM((2, 128, H - EARLY), BF16),
            pltpu.VMEM((4, 2, 128, EARLY), BF16),
            pltpu.VMEM((512, D), F32),
            pltpu.VMEM((512, D), BF16),
            pltpu.VMEM((512, D), BF16),
            pltpu.VMEM((128, D), F32),
            pltpu.VMEM((4, 128, D), BF16),
            pltpu.VMEM((4, 128, D), BF16),
            pltpu.VMEM((32, D), F32),
            pltpu.VMEM((4, 32, D), BF16),
            pltpu.VMEM((4, 32, D), BF16),
            pltpu.VMEM((N_DP, 4, D), F32),
            pltpu.VMEM((N_DP, 4, D), F32),
            dma((3,)),
            dma((N_EX,)),
            dma((N_EX,)),
            dma((N_EX,)),
            dma((N_EX,)),
            dma((4, 2)),
            dma((4, 2)),
            dma((N_EX,)),
            dma((N_EX,)),
            dma((2, 6)),
            dma((2, 6)),
            dma((2,)),
            dma((2,)),
            dma((1,)),
            dma((1,)),
            dma((4,)),
            dma((4,)),
            dma((4,)),
            dma((4,)),
            dma((N_DP,)),
            dma((N_DP,)),
        ],
        compiler_params=pltpu.CompilerParams(
            collective_id=0, has_side_effects=True, vmem_limit_bytes=62 << 20
        ),
    )(
        cell_rows.reshape(ALL_ROWS, D),
        cotangent.reshape(ALL_ROWS, D),
        cluster_ids.reshape(MICRO, ROWS),
        enc_weight,
        up_weight,
        down_weight,
    )
    return pl.pallas_call(
        settle,
        name="settle",
        out_shape=tuple(jax.ShapeDtypeStruct(o.shape, o.dtype) for o in outs),
        in_specs=[vmem] * 3,
        out_specs=(vmem,) * 3,
    )(*outs)


def solution(mesh):
    in_specs = (
        P(None, ("dp", "expert"), None),
        P(None, ("dp", "expert"), None),
        P(None, ("dp", "expert"), None),
        P(),
        P("expert", None, None),
        P("expert", None, None),
    )
    out_specs = (P(("dp", "expert"), None), P("expert", "dp", None), P("expert", "dp", None))
    return jax.shard_map(body, mesh=mesh, in_specs=in_specs, out_specs=out_specs, check_vma=False)
```

```python
import jax
import jax.numpy as jnp
from jax import lax
from jax.experimental import pallas as pl
from jax.experimental.pallas import tpu as pltpu
from jax.sharding import PartitionSpec as P

MESH = pl.DeviceIdType.MESH
F32 = jnp.float32
BF16 = jnp.bfloat16
epsilon = 1e-06

N_DP = 8
N_EX = 32
D = 1024
H = 2048
ROWS = 128
MICRO = 2
ALL_ROWS = MICRO * ROWS
CAP = 8
SLOT = MICRO * CAP
SLOTS = N_EX * SLOT
WIDE = 512
EARLY = 256


def dot(a, b):
    return jnp.dot(a, b, preferred_element_type=F32)


def dot_nt(a, b):
    return lax.dot_general(a, b, (((1,), (1,)), ((), ())), preferred_element_type=F32)


def dot_tn(a, b):
    return lax.dot_general(a, b, (((0,), (0,)), ((), ())), preferred_element_type=F32)


def aligned(index, size):
    return pl.ds(pl.multiple_of(index * size, size), size)


def loop(low, high, step):
    def body(index, carry):
        step(index)
        return carry

    lax.fori_loop(low, high, body, 0)


def kernel(
    cell, cot, ids, encw_hbm, up_hbm, down_hbm,
    enc_out, up_out, down_out,
    encw, w_up, w_down, normed, send_n, send_g, recv_n, recv_g, pre_grad, active, back, ret,
    enc_s, slope_s, inv_s, placer, fperm, egrad,
    part, rs_recv, z_recv, early_recv,
    e_own, e_send, e_recv, x_own, x_send, x_recv, h_own, h_send, h_recv, d_send, d_recv,
    w_sem, disp_s, disp_r, dispg_s, dispg_r, early_s, early_r, ret_s, ret_r, rs_s, rs_r, z_s, z_r, c_s, c_r, x_s, x_r, h_s, h_r, d_s, d_r,
):
    d = lax.axis_index("dp")
    e = lax.axis_index("expert")
    z_lo, y = d // 4, d % 4
    z_hi, plane = e // 8, e % 8
    x, core = plane // 2, plane % 2
    right = (z_lo * 4 + (y + 1) % 4, e)
    left = (z_lo * 4 + (y + 3) % 4, e)
    mate = ((1 - z_lo) * 4 + y, e)

    def copy(src, dst, s, r, who):
        return pltpu.make_async_remote_copy(
            src_ref=src, dst_ref=dst, send_sem=s, recv_sem=r, device_id=who, device_id_type=MESH
        )

    enc_copy = pltpu.make_async_copy(encw_hbm, encw, w_sem.at[2])
    enc_copy.start()
    w_copies = [
        pltpu.make_async_copy(up_hbm.at[0], w_up, w_sem.at[0]),
        pltpu.make_async_copy(down_hbm.at[0], w_down, w_sem.at[1]),
    ]
    for item in w_copies:
        item.start()

    barrier = pltpu.get_barrier_semaphore()

    def greet_expert(k):
        pl.semaphore_signal(barrier, inc=1, device_id=(d, (e + k) % N_EX), device_id_type=MESH)

    def greet_dp(k):
        pl.semaphore_signal(barrier, inc=1, device_id=((d + k) % N_DP, e), device_id_type=MESH)

    loop(1, N_EX, greet_expert)
    loop(1, N_DP, greet_dp)

    upper = (
        lax.broadcasted_iota(jnp.int32, (ROWS, ROWS), 0) < lax.broadcasted_iota(jnp.int32, (ROWS, ROWS), 1)
    ).astype(F32).astype(BF16)
    for m in range(MICRO):
        label = ids[m : m + 1, :]
        onehot = (label == lax.broadcasted_iota(jnp.int32, (N_EX, ROWS), 0)).astype(F32)
        before = dot(onehot.astype(BF16), upper)
        rank = jnp.sum(before * onehot, axis=0, keepdims=True).astype(jnp.int32)
        target = label * SLOT + m * CAP + rank
        slots = lax.broadcasted_iota(jnp.int32, (SLOTS, ROWS), 0)
        placer[:, m * ROWS : (m + 1) * ROWS] = (slots == target).astype(F32).astype(BF16)

    def to_g(c):
        return copy(send_g.at[aligned(c, SLOT), :], recv_g.at[aligned(e, SLOT), :], dispg_s.at[c], dispg_r.at[e], (d, c))

    def from_g(c):
        return copy(send_g.at[aligned(c, SLOT), :], recv_g.at[aligned(c, SLOT), :], dispg_s.at[c], dispg_r.at[c], (d, c))

    def to_n(c):
        return copy(send_n.at[aligned(c, SLOT), :], recv_n.at[aligned(e, SLOT), :], disp_s.at[c], disp_r.at[e], (d, c))

    def from_n(c):
        return copy(send_n.at[aligned(c, SLOT), :], recv_n.at[aligned(c, SLOT), :], disp_s.at[c], disp_r.at[c], (d, c))

    order = (0, 1, 3, 2)
    far_first = (1, 3, 2, 0)

    def peer(hop, k):
        return ((z_hi + hop) % 4) * 8 + (plane + k) % 8

    def peers(hop, step):
        loop(1 if hop == 0 else 0, 8, lambda k: step(peer(hop, k)))

    for hop in far_first:
        group = aligned((z_hi + hop) % 4, 128)
        send_g[group, :] = dot(placer[group, :], cot[...]).astype(BF16)
        if hop == far_first[0]:
            pl.semaphore_wait(barrier, N_EX + N_DP - 2)
        peers(hop, lambda c: to_g(c).start())
    recv_g[aligned(e, SLOT), :] = send_g[aligned(e, SLOT), :]

    inv_s[...] = jnp.zeros_like(inv_s)
    enc_copy.wait()

    def encode(n):
        cols = aligned(n, 256)
        pre = dot(cell[...], encw[:, cols])
        gate = jax.nn.sigmoid(pre)
        encoded = cell[:, cols].astype(F32) + pre * gate
        enc_s[:, cols] = encoded
        slope_s[:, cols] = gate * (1.0 + pre * (1.0 - gate))
        square = encoded * encoded
        inv_s[...] += square[:, :128] + square[:, 128:]

    loop(0, 4, encode)

    def normalize(i):
        rows = aligned(i, 64)
        inverse = lax.rsqrt(jnp.sum(inv_s[rows, :], axis=1, keepdims=True) * (1.0 / D) + epsilon)
        inv_s[rows, :] = jnp.broadcast_to(inverse, (64, 128))
        normed[rows, :] = (enc_s[rows, :] * inverse).astype(BF16)

    loop(0, 4, normalize)
    for hop in far_first:
        group = aligned((z_hi + hop) % 4, 128)
        send_n[group, :] = dot(placer[group, :], normed[...]).astype(BF16)
        peers(hop, lambda c: to_n(c).start())
    recv_n[aligned(e, SLOT), :] = send_n[aligned(e, SLOT), :]

    def permute(n):
        col = lax.broadcasted_iota(jnp.int32, (1, 256), 1) + n * 256
        nat = (
            (col & 3)
            + (((col >> 2) & 7) << 7)
            + (((col >> 5) & 3) << 5)
            + (((col >> 7) & 3) << 3)
            + ((col >> 9) << 2)
        )
        pick = (lax.broadcasted_iota(jnp.int32, (D, 256), 0) == nat).astype(F32).astype(BF16)
        fperm[:, aligned(n, 256)] = dot(cell[...], pick).astype(BF16)

    loop(0, 4, permute)
    for item in w_copies:
        item.wait()

    def give_back(c):
        return copy(back.at[aligned(c, SLOT), :], ret.at[aligned(e, SLOT), :], ret_s.at[c], ret_r.at[e], (d, c))

    def came_back(c):
        return copy(back.at[aligned(c, SLOT), :], ret.at[aligned(c, SLOT), :], ret_s.at[c], ret_r.at[c], (d, c))

    def mlp(hop):
        group = aligned((z_hi + hop) % 4, 128)
        peers(hop, lambda c: from_g(c).wait_recv())
        peers(hop, lambda c: from_n(c).wait_recv())
        if hop == order[-1]:
            for earlier in order[1:-1]:
                peers(earlier, lambda c: give_back(c).start())

        def hidden(n):
            cols = aligned(n, WIDE)
            pre = dot(recv_n[group, :], w_up[:, cols])
            act_grad = dot(recv_g[group, :], w_down[:, cols])
            gate = jax.nn.sigmoid(pre)
            active[group, cols] = (pre * gate).astype(BF16)
            pre_grad[group, cols] = (act_grad * (gate * (1.0 + pre * (1.0 - gate)))).astype(BF16)

        loop(0, H // WIDE, hidden)

    def mlp_back(hop):
        group = aligned((z_hi + hop) % 4, 128)

        def backward(n):
            back[group, aligned(n, 256)] = dot_nt(pre_grad[group, :], w_up[aligned(n, 256), :]).astype(BF16)

        loop(0, D // 256, backward)

    for hop in order:
        mlp(hop)
        if hop != order[-1]:
            mlp_back(hop)
        if hop == 0:
            peers(0, lambda c: give_back(c).start())

    def grads(p, q):
        block = ((1 - z_lo) if p == 0 else z_lo) * 4 + (y + (2, 1, 3, 0)[q]) % 4
        up_t = recv_n[:, aligned(block, 128)].T
        down_t = recv_g[:, aligned(block, 128)].T

        def piece(n):
            cols = aligned(n, WIDE)
            part[p, q, 0, :, cols] = dot(up_t, pre_grad[:, cols]).astype(BF16)
            part[p, q, 1, :, cols] = dot(down_t, active[:, cols]).astype(BF16)

        loop(0, H // WIDE, piece)

    late = (pl.ds(EARLY, H - EARLY), pl.ds(0, H))

    def rs(p, slot):
        q, which, who = ((0, 0, right), (0, 1, left), (1, 1, right), (2, 0, left), (1, 0, right), (2, 1, left))[slot]
        return copy(
            part.at[p, q, which, :, late[p]], rs_recv.at[p, slot, :, late[p]], rs_s.at[p, slot], rs_r.at[p, slot], who
        )

    def early(q, w):
        return copy(
            part.at[0, q, w, :, pl.ds(0, EARLY)], early_recv.at[q, w], early_s.at[q, w], early_r.at[q, w], mate
        )

    def add_early(q):
        for w in range(2):
            early(q, w).wait_recv()

            def piece(n):
                rows = aligned(n, 64)
                total = part[1, q, w, rows, :EARLY].astype(F32) + early_recv[q, w, rows, :].astype(F32)
                part[1, q, w, rows, :EARLY] = total.astype(BF16)

            loop(0, 2, piece)

    def add_into(p, q, which, others):
        def piece(n):
            rows = aligned(n, 32)
            total = part[p, q, which, rows, late[p]].astype(F32)
            for slot in others:
                total = total + rs_recv[p, slot, rows, late[p]].astype(F32)
            part[p, q, which, rows, late[p]] = total.astype(BF16)

        loop(0, 4, piece)

    def combine(p):
        rs(p, 0).wait_recv()
        add_into(p, 1, 0, (0,))
        rs(p, 4).start()
        rs(p, 1).wait_recv()
        add_into(p, 2, 1, (1,))
        rs(p, 5).start()

    grads(0, 0)
    rs(0, 0).start()
    rs(0, 1).start()
    mlp_back(order[-1])
    peers(order[-1], lambda c: give_back(c).start())
    ret[aligned(e, SLOT), :] = back[aligned(e, SLOT), :]
    for q in (1, 2, 3):
        grads(0, q)
        if q < 3:
            rs(0, q + 1).start()
    for q in range(4):
        early(q, 0).start()
        early(q, 1).start()
    combine(0)
    for q in range(4):
        grads(1, q)

    for hop in order:
        peers(hop, lambda c: came_back(c).wait_recv())

    def encoder_back(i):
        rows = aligned(i, 128)
        norm_grad = dot_tn(placer[:, rows], ret[...])
        encoded = enc_s[rows, :]
        inverse = inv_s[rows, 0:1]
        mean = jnp.sum(norm_grad * encoded, axis=1, keepdims=True) * (1.0 / D)
        grad = inverse * norm_grad - inverse * inverse * inverse * encoded * mean
        egrad[rows, :] = (grad * slope_s[rows, :]).astype(BF16)

    loop(0, 2, encoder_back)

    def enc_piece(index):
        return dot(fperm[:, aligned(index, 128)].T, egrad[...])

    def enc_other(n):
        e_send[aligned(n, 128), :] = enc_piece((1 - core) * 4 + n).astype(BF16)

    def enc_own(n):
        e_own[aligned(n, 128), :] = enc_piece(core * 4 + n)

    loop(0, 4, enc_other)
    to_core = copy(e_send, e_recv, c_s.at[0], c_r.at[0], (d, e + 1 - 2 * core))
    to_core.start()
    loop(0, 4, enc_own)

    to_core.wait_recv()

    def x_device(k):
        return (x + k) % 4

    def x_copy(k):
        to = x_device(k)
        return copy(x_send.at[to], x_recv.at[x], x_s.at[to], x_r.at[x], (d, (z_hi * 4 + to) * 2 + core))

    def x_from(k):
        to = x_device(k)
        return copy(x_send.at[to], x_recv.at[to], x_s.at[to], x_r.at[to], (d, (z_hi * 4 + to) * 2 + core))

    for k in (2, 1, 3):
        rows = aligned(x_device(k), 128)
        x_send[x_device(k)] = (e_own[rows, :] + e_recv[rows, :].astype(F32)).astype(BF16)
        x_copy(k).start()
    rows = aligned(x, 128)
    x_own[...] = e_own[rows, :] + e_recv[rows, :].astype(F32)

    add_early(0)
    rs(1, 0).start()
    rs(1, 1).start()
    add_early(1)
    rs(1, 2).start()
    add_early(2)
    rs(1, 3).start()
    add_early(3)

    def finish(p, w):
        for slot in ((3, 4), (2, 5))[w]:
            rs(p, slot).wait_recv()

    to_mate = [
        copy(part.at[0, 3, w, :, late[0]], z_recv.at[w], z_s.at[w], z_r.at[w], mate) for w in range(2)
    ]
    finish(0, 0)
    add_into(0, 3, 0, (3, 4))
    to_mate[0].start()

    for k in (1, 3, 2):
        x_from(k).wait_recv()

    def h_copy(k):
        to = (z_hi + k) % 4
        return copy(h_send.at[to], h_recv.at[z_hi], h_s.at[to], h_r.at[z_hi], (d, to * 8 + plane))

    def h_from(k):
        to = (z_hi + k) % 4
        return copy(h_send.at[to], h_recv.at[to], h_s.at[to], h_r.at[to], (d, to * 8 + plane))

    def x_sum(to):
        rows = aligned(to, 32)
        total = x_own[rows, :]
        for k in (1, 2, 3):
            total = total + x_recv[x_device(k), rows, :].astype(F32)
        return total

    for k in (2, 1, 3):
        h_send[(z_hi + k) % 4] = x_sum((z_hi + k) % 4).astype(BF16)
        h_copy(k).start()
    h_own[...] = x_sum(z_hi)
    finish(0, 1)
    add_into(0, 3, 1, (2, 5))
    to_mate[1].start()
    combine(1)
    for k in (1, 3, 2):
        h_from(k).wait_recv()
    total = h_own[...]
    for k in (1, 2, 3):
        total = total + h_recv[(z_hi + k) % 4].astype(F32)
    d_send[...] = total.reshape(N_DP, 4, D)

    def d_copy(k):
        to = (d + k) % N_DP
        return copy(d_send.at[to], d_recv.at[d], d_s.at[to], d_r.at[d], (to, e))

    def d_from(k):
        to = (d + k) % N_DP
        return copy(d_send.at[to], d_recv.at[to], d_s.at[to], d_r.at[to], (to, e))

    loop(1, N_DP, lambda k: d_copy(k).start())

    for w, (out, others) in enumerate(((up_out, (3, 4)), (down_out, (2, 5)))):
        to_mate[w].wait_recv()
        finish(1, w)

        def piece(n):
            rows = aligned(n, 32)
            total = part[1, 3, w, rows, :].astype(F32)
            for slot in others:
                total = total + rs_recv[1, slot, rows, :].astype(F32)
            out[0, rows, :EARLY] = total[:, :EARLY].astype(BF16)
            out[0, rows, EARLY:] = (total[:, EARLY:] + z_recv[w, rows, :].astype(F32)).astype(BF16)

        loop(0, 4, piece)

    loop(1, N_DP, lambda k: d_from(k).wait_recv())
    total = d_send[d]
    for k in range(1, N_DP):
        total = total + d_recv[(d + k) % N_DP]
    enc_out[...] = total

    for hop in order:
        peers(hop, lambda c: to_g(c).wait_send())
        peers(hop, lambda c: to_n(c).wait_send())
        peers(hop, lambda c: give_back(c).wait_send())
    for p in range(2):
        for slot in range(6):
            rs(p, slot).wait_send()
    for w in range(2):
        to_mate[w].wait_send()
        for q in range(4):
            early(q, w).wait_send()
    to_core.wait_send()
    for k in (1, 2, 3):
        x_copy(k).wait_send()
        h_copy(k).wait_send()
    loop(1, N_DP, lambda k: d_copy(k).wait_send())


def settle(enc_in, up_in, down_in, enc_out, up_out, down_out):
    enc_out[...] = enc_in[...]
    up_out[...] = up_in[...]
    down_out[...] = down_in[...]


def body(cell_rows, cotangent, cluster_ids, enc_weight, up_weight, down_weight):
    vmem = pl.BlockSpec(memory_space=pltpu.VMEM)
    hbm = pl.BlockSpec(memory_space=pl.ANY)
    dma = pltpu.SemaphoreType.DMA
    outs = pl.pallas_call(
        kernel,
        name="step",
        out_shape=(
            jax.ShapeDtypeStruct((4, D), F32),
            jax.ShapeDtypeStruct((1, 128, H), BF16),
            jax.ShapeDtypeStruct((1, 128, H), BF16),
        ),
        in_specs=[vmem, vmem, vmem, hbm, hbm, hbm],
        out_specs=(vmem, vmem, vmem),
        scratch_shapes=[
            pltpu.VMEM((D, D), BF16),
            pltpu.VMEM((D, H), BF16),
            pltpu.VMEM((D, H), BF16),
            pltpu.VMEM((ALL_ROWS, D), BF16),
            pltpu.VMEM((SLOTS, D), BF16),
            pltpu.VMEM((SLOTS, D), BF16),
            pltpu.VMEM((SLOTS, D), BF16),
            pltpu.VMEM((SLOTS, D), BF16),
            pltpu.VMEM((SLOTS, H), BF16),
            pltpu.VMEM((SLOTS, H), BF16),
            pltpu.VMEM((SLOTS, D), BF16),
            pltpu.VMEM((SLOTS, D), BF16),
            pltpu.VMEM((ALL_ROWS, D), F32),
            pltpu.VMEM((ALL_ROWS, D), F32),
            pltpu.VMEM((ALL_ROWS, 128), F32),
            pltpu.VMEM((SLOTS, ALL_ROWS), BF16),
            pltpu.VMEM((ALL_ROWS, D), BF16),
            pltpu.VMEM((ALL_ROWS, D), BF16),
            pltpu.VMEM((2, 4, 2, 128, H), BF16),
            pltpu.VMEM((2, 6, 128, H), BF16),
            pltpu.VMEM((2, 128, H - EARLY), BF16),
            pltpu.VMEM((4, 2, 128, EARLY), BF16),
            pltpu.VMEM((512, D), F32),
            pltpu.VMEM((512, D), BF16),
            pltpu.VMEM((512, D), BF16),
            pltpu.VMEM((128, D), F32),
            pltpu.VMEM((4, 128, D), BF16),
            pltpu.VMEM((4, 128, D), BF16),
            pltpu.VMEM((32, D), F32),
            pltpu.VMEM((4, 32, D), BF16),
            pltpu.VMEM((4, 32, D), BF16),
            pltpu.VMEM((N_DP, 4, D), F32),
            pltpu.VMEM((N_DP, 4, D), F32),
            dma((3,)),
            dma((N_EX,)),
            dma((N_EX,)),
            dma((N_EX,)),
            dma((N_EX,)),
            dma((4, 2)),
            dma((4, 2)),
            dma((N_EX,)),
            dma((N_EX,)),
            dma((2, 6)),
            dma((2, 6)),
            dma((2,)),
            dma((2,)),
            dma((1,)),
            dma((1,)),
            dma((4,)),
            dma((4,)),
            dma((4,)),
            dma((4,)),
            dma((N_DP,)),
            dma((N_DP,)),
        ],
        compiler_params=pltpu.CompilerParams(
            collective_id=0, has_side_effects=True, vmem_limit_bytes=62 << 20
        ),
    )(
        cell_rows.reshape(ALL_ROWS, D),
        cotangent.reshape(ALL_ROWS, D),
        cluster_ids.reshape(MICRO, ROWS),
        enc_weight,
        up_weight,
        down_weight,
    )
    return pl.pallas_call(
        settle,
        name="settle",
        out_shape=tuple(jax.ShapeDtypeStruct(o.shape, o.dtype) for o in outs),
        in_specs=[vmem] * 3,
        out_specs=(vmem,) * 3,
    )(*outs)


def solution(mesh):
    in_specs = (
        P(None, ("dp", "expert"), None),
        P(None, ("dp", "expert"), None),
        P(None, ("dp", "expert"), None),
        P(),
        P("expert", None, None),
        P("expert", None, None),
    )
    out_specs = (P(("dp", "expert"), None), P("expert", "dp", None), P("expert", "dp", None))
    return jax.shard_map(body, mesh=mesh, in_specs=in_specs, out_specs=out_specs, check_vma=False)
```

```python
import jax
import jax.numpy as jnp
from jax import lax
from jax.experimental import pallas as pl
from jax.experimental.pallas import tpu as pltpu
from jax.sharding import PartitionSpec as P

MESH = pl.DeviceIdType.MESH
F32 = jnp.float32
BF16 = jnp.bfloat16
epsilon = 1e-06

N_DP = 8
N_EX = 32
D = 1024
H = 2048
ROWS = 128
MICRO = 2
ALL_ROWS = MICRO * ROWS
CAP = 8
SLOT = MICRO * CAP
SLOTS = N_EX * SLOT
WIDE = 512
EARLY = 512


def dot(a, b):
    return jnp.dot(a, b, preferred_element_type=F32)


def dot_nt(a, b):
    return lax.dot_general(a, b, (((1,), (1,)), ((), ())), preferred_element_type=F32)


def dot_tn(a, b):
    return lax.dot_general(a, b, (((0,), (0,)), ((), ())), preferred_element_type=F32)


def aligned(index, size):
    return pl.ds(pl.multiple_of(index * size, size), size)


def loop(low, high, step):
    def body(index, carry):
        step(index)
        return carry

    lax.fori_loop(low, high, body, 0)


def kernel(
    cell, cot, ids, encw_hbm, up_hbm, down_hbm,
    enc_out, up_out, down_out,
    encw, w_up, w_down, held, normed, send_n, send_g, recv_n, recv_g, pre_grad, active, back, ret,
    enc_s, slope_s, inv_s, placer, fperm, egrad,
    part, rs_recv, z_recv, early_recv,
    e_own, e_send, e_recv, x_own, x_send, x_recv, h_own, h_send, h_recv, d_send, d_recv,
    w_sem, disp_s, disp_r, dispg_s, dispg_r, early_s, early_r, ret_s, ret_r, rs_s, rs_r, z_s, z_r, c_s, c_r, x_s, x_r, h_s, h_r, d_s, d_r,
):
    d = lax.axis_index("dp")
    e = lax.axis_index("expert")
    z_lo, y = d // 4, d % 4
    z_hi, plane = e // 8, e % 8
    x, core = plane // 2, plane % 2
    right = (z_lo * 4 + (y + 1) % 4, e)
    left = (z_lo * 4 + (y + 3) % 4, e)
    mate = ((1 - z_lo) * 4 + y, e)

    def copy(src, dst, s, r, who):
        return pltpu.make_async_remote_copy(
            src_ref=src, dst_ref=dst, send_sem=s, recv_sem=r, device_id=who, device_id_type=MESH
        )

    enc_copy = pltpu.make_async_copy(encw_hbm, encw, w_sem.at[2])
    enc_copy.start()
    w_copies = [
        pltpu.make_async_copy(up_hbm.at[0], w_up, w_sem.at[0]),
        pltpu.make_async_copy(down_hbm.at[0], w_down, w_sem.at[1]),
    ]
    for item in w_copies:
        item.start()

    barrier = pltpu.get_barrier_semaphore()

    def greet_plane(k):
        index = z_lo * N_EX + e + k
        who = (((index // N_EX) % 2) * 4 + y, index % N_EX)
        pl.semaphore_signal(barrier, inc=1, device_id=who, device_id_type=MESH)

    def greet_ring(k):
        for half in range(2):
            who = (half * 4 + (y + k) % 4, e)
            pl.semaphore_signal(barrier, inc=1, device_id=who, device_id_type=MESH)

    loop(1, 2 * N_EX, greet_plane)
    loop(1, 4, greet_ring)

    upper = (
        lax.broadcasted_iota(jnp.int32, (ROWS, ROWS), 0) < lax.broadcasted_iota(jnp.int32, (ROWS, ROWS), 1)
    ).astype(F32).astype(BF16)
    for m in range(MICRO):
        label = ids[m : m + 1, :]
        onehot = (label == lax.broadcasted_iota(jnp.int32, (N_EX, ROWS), 0)).astype(F32)
        before = dot(onehot.astype(BF16), upper)
        rank = jnp.sum(before * onehot, axis=0, keepdims=True).astype(jnp.int32)
        target = label * SLOT + m * CAP + rank
        slots = lax.broadcasted_iota(jnp.int32, (SLOTS, ROWS), 0)
        placer[:, m * ROWS : (m + 1) * ROWS] = (slots == target).astype(F32).astype(BF16)

    def near(hop):
        return (z_lo, 0, 1 - z_lo, 1)[hop]

    def place(hop):
        group = (0, 1 + 2 * z_lo, 2, 1 + 2 * z_lo)[hop]
        return group * 8 + plane

    beside = (z_hi + 3 + 2 * z_lo) % 4

    def source(group, k):
        half, high = ((z_lo, z_hi), (0, beside), (1 - z_lo, (z_hi + 2) % 4), (1, beside))[group]
        other = (plane + k) % 8
        return group * 8 + other, (half * 4 + y, high * 8 + other)

    def target(hop, k):
        cluster = ((z_hi + hop) % 4) * 8 + (plane + k) % 8
        return cluster, (near(hop) * 4 + y, cluster)

    def sending(hop, k, src, dst, s, r):
        cluster, who = target(hop, k)
        at = place(hop)
        return copy(src.at[aligned(cluster, SLOT), :], dst.at[aligned(at, SLOT), :], s.at[cluster], r.at[at], who)

    def landing(group, k, src, dst, s, r):
        at, who = source(group, k)
        return copy(src.at[aligned(at, SLOT), :], dst.at[aligned(at, SLOT), :], s.at[at], r.at[at], who)

    def to_g(hop, k):
        return sending(hop, k, send_g, recv_g, dispg_s, dispg_r)

    def from_g(group, k):
        return landing(group, k, send_g, recv_g, dispg_s, dispg_r)

    def to_n(hop, k):
        return sending(hop, k, send_n, recv_n, disp_s, disp_r)

    def from_n(group, k):
        return landing(group, k, send_n, recv_n, disp_s, disp_r)

    def give_back(group, k):
        at, who = source(group, k)
        return copy(back.at[aligned(at, SLOT), :], ret.at[aligned(e, SLOT), :], ret_s.at[at], ret_r.at[e], who)

    def came_back(hop, k):
        cluster, who = target(hop, k)
        rows = aligned(cluster, SLOT)
        return copy(back.at[rows, :], ret.at[rows, :], ret_s.at[cluster], ret_r.at[cluster], who)

    order = (0, 1, 3, 2)
    far_first = (1, 3, 2, 0)

    def peers(index, step):
        loop(1 if index == 0 else 0, 8, lambda k: step(index, k))

    for hop in far_first:
        group = aligned((z_hi + hop) % 4, 128)
        send_g[group, :] = dot(placer[group, :], cot[...]).astype(BF16)
        if hop == far_first[0]:
            pl.semaphore_wait(barrier, 2 * N_EX - 1 + 6)
        peers(hop, lambda h, k: to_g(h, k).start())
    recv_g[aligned(plane, SLOT), :] = send_g[aligned(e, SLOT), :]

    inv_s[...] = jnp.zeros_like(inv_s)
    enc_copy.wait()

    def encode(n):
        cols = aligned(n, 256)
        pre = dot(cell[...], encw[:, cols])
        gate = jax.nn.sigmoid(pre)
        encoded = cell[:, cols].astype(F32) + pre * gate
        enc_s[:, cols] = encoded
        slope_s[:, cols] = gate * (1.0 + pre * (1.0 - gate))
        square = encoded * encoded
        inv_s[...] += square[:, :128] + square[:, 128:]

    loop(0, 4, encode)

    def normalize(i):
        rows = aligned(i, 64)
        inverse = lax.rsqrt(jnp.sum(inv_s[rows, :], axis=1, keepdims=True) * (1.0 / D) + epsilon)
        inv_s[rows, :] = jnp.broadcast_to(inverse, (64, 128))
        normed[rows, :] = (enc_s[rows, :] * inverse).astype(BF16)

    loop(0, 4, normalize)
    for hop in far_first:
        group = aligned((z_hi + hop) % 4, 128)
        send_n[group, :] = dot(placer[group, :], normed[...]).astype(BF16)
        peers(hop, lambda h, k: to_n(h, k).start())
    recv_n[aligned(plane, SLOT), :] = send_n[aligned(e, SLOT), :]

    def permute(n):
        col = lax.broadcasted_iota(jnp.int32, (1, 256), 1) + n * 256
        nat = (
            (col & 3)
            + (((col >> 2) & 7) << 7)
            + (((col >> 5) & 3) << 5)
            + (((col >> 7) & 3) << 3)
            + ((col >> 9) << 2)
        )
        pick = (lax.broadcasted_iota(jnp.int32, (D, 256), 0) == nat).astype(F32).astype(BF16)
        fperm[:, aligned(n, 256)] = dot(cell[...], pick).astype(BF16)

    loop(0, 4, permute)
    for item in w_copies:
        item.wait()

    def silu_and_grad(group, cols, act_grad):
        pre = dot(recv_n[group, :], w_up[:, cols])
        gate = jax.nn.sigmoid(pre)
        active[group, cols] = (pre * gate).astype(BF16)
        pre_grad[group, cols] = (act_grad * (gate * (1.0 + pre * (1.0 - gate)))).astype(BF16)

    def mlp(index):
        group = pl.ds(index * 128, 128)
        peers(index, lambda g, k: from_g(g, k).wait_recv())
        peers(index, lambda g, k: from_n(g, k).wait_recv())

        def hidden(n):
            cols = aligned(n, WIDE)
            silu_and_grad(group, cols, dot(recv_g[group, :], w_down[:, cols]))

        loop(0, H // WIDE, hidden)

    def mlp_last(index):
        group = pl.ds(index * 128, 128)
        peers(index, lambda g, k: from_g(g, k).wait_recv())

        def first(n):
            cols = aligned(n, WIDE)
            held[:, cols] = dot(recv_g[group, :], w_down[:, cols])

        loop(0, H // WIDE, first)
        peers(index, lambda g, k: from_n(g, k).wait_recv())
        for earlier in order[1:-1]:
            peers(earlier, lambda g, k: give_back(g, k).start())

        def hidden(n):
            cols = aligned(n, WIDE)
            silu_and_grad(group, cols, held[:, cols])

        loop(0, H // WIDE, hidden)

    def mlp_back(index):
        group = pl.ds(index * 128, 128)

        def backward(n):
            back[group, aligned(n, 256)] = dot_nt(pre_grad[group, :], w_up[aligned(n, 256), :]).astype(BF16)

        loop(0, D // 256, backward)

    for index in order[:-1]:
        mlp(index)
        mlp_back(index)
        if index == 0:
            peers(0, lambda g, k: give_back(g, k).start())
    mlp_last(order[-1])

    def grads(p, q):
        block = ((1 - z_lo) if p == 0 else z_lo) * 4 + (y + (2, 1, 3, 0)[q]) % 4
        up_t = recv_n[:, aligned(block, 128)].T
        down_t = recv_g[:, aligned(block, 128)].T

        def piece(n):
            cols = aligned(n, WIDE)
            part[p, q, 0, :, cols] = dot(up_t, pre_grad[:, cols]).astype(BF16)
            part[p, q, 1, :, cols] = dot(down_t, active[:, cols]).astype(BF16)

        loop(0, H // WIDE, piece)

    late = (pl.ds(EARLY, H - EARLY), pl.ds(0, H))

    def rs(p, slot):
        q, which, who = ((0, 0, right), (0, 1, left), (1, 1, right), (2, 0, left), (1, 0, right), (2, 1, left))[slot]
        return copy(
            part.at[p, q, which, :, late[p]], rs_recv.at[p, slot, :, late[p]], rs_s.at[p, slot], rs_r.at[p, slot], who
        )

    def early(q, w):
        return copy(
            part.at[0, q, w, :, pl.ds(0, EARLY)], early_recv.at[q, w], early_s.at[q, w], early_r.at[q, w], mate
        )

    def add_early(q):
        for w in range(2):
            early(q, w).wait_recv()

            def piece(n):
                rows = aligned(n, 64)
                total = part[1, q, w, rows, :EARLY].astype(F32) + early_recv[q, w, rows, :].astype(F32)
                part[1, q, w, rows, :EARLY] = total.astype(BF16)

            loop(0, 2, piece)

    def add_into(p, q, which, others):
        def piece(n):
            rows = aligned(n, 32)
            total = part[p, q, which, rows, late[p]].astype(F32)
            for slot in others:
                total = total + rs_recv[p, slot, rows, late[p]].astype(F32)
            part[p, q, which, rows, late[p]] = total.astype(BF16)

        loop(0, 4, piece)

    def combine(p):
        rs(p, 0).wait_recv()
        add_into(p, 1, 0, (0,))
        rs(p, 4).start()
        rs(p, 1).wait_recv()
        add_into(p, 2, 1, (1,))
        rs(p, 5).start()

    grads(0, 0)
    rs(0, 0).start()
    rs(0, 1).start()
    early(0, 0).start()
    early(0, 1).start()
    mlp_back(order[-1])
    peers(order[-1], lambda g, k: give_back(g, k).start())
    ret[aligned(e, SLOT), :] = back[aligned(plane, SLOT), :]
    for q in (1, 2, 3):
        grads(0, q)
        if q < 3:
            rs(0, q + 1).start()
        early(q, 0).start()
        early(q, 1).start()
    combine(0)
    grads(1, 0)
    add_early(0)
    rs(1, 0).start()
    rs(1, 1).start()
    for q in (1, 2, 3):
        grads(1, q)

    for hop in order:
        peers(hop, lambda h, k: came_back(h, k).wait_recv())

    def encoder_back(i):
        rows = aligned(i, 128)
        norm_grad = dot_tn(placer[:, rows], ret[...])
        encoded = enc_s[rows, :]
        inverse = inv_s[rows, 0:1]
        mean = jnp.sum(norm_grad * encoded, axis=1, keepdims=True) * (1.0 / D)
        grad = inverse * norm_grad - inverse * inverse * inverse * encoded * mean
        egrad[rows, :] = (grad * slope_s[rows, :]).astype(BF16)

    loop(0, 2, encoder_back)

    def enc_piece(index):
        return dot(fperm[:, aligned(index, 128)].T, egrad[...])

    def enc_other(n):
        e_send[aligned(n, 128), :] = enc_piece((1 - core) * 4 + n).astype(BF16)

    def enc_own(n):
        e_own[aligned(n, 128), :] = enc_piece(core * 4 + n)

    loop(0, 4, enc_other)
    to_core = copy(e_send, e_recv, c_s.at[0], c_r.at[0], (d, e + 1 - 2 * core))
    to_core.start()
    loop(0, 4, enc_own)

    to_core.wait_recv()

    def x_device(k):
        return (x + k) % 4

    def x_copy(k):
        to = x_device(k)
        return copy(x_send.at[to], x_recv.at[x], x_s.at[to], x_r.at[x], (d, (z_hi * 4 + to) * 2 + core))

    def x_from(k):
        to = x_device(k)
        return copy(x_send.at[to], x_recv.at[to], x_s.at[to], x_r.at[to], (d, (z_hi * 4 + to) * 2 + core))

    for k in (2, 1, 3):
        rows = aligned(x_device(k), 128)
        x_send[x_device(k)] = (e_own[rows, :] + e_recv[rows, :].astype(F32)).astype(BF16)
        x_copy(k).start()
    rows = aligned(x, 128)
    x_own[...] = e_own[rows, :] + e_recv[rows, :].astype(F32)

    add_early(1)
    rs(1, 2).start()
    add_early(2)
    rs(1, 3).start()
    add_early(3)

    def finish(p, w):
        for slot in ((3, 4), (2, 5))[w]:
            rs(p, slot).wait_recv()

    to_mate = [
        copy(part.at[0, 3, w, :, late[0]], z_recv.at[w], z_s.at[w], z_r.at[w], mate) for w in range(2)
    ]
    finish(0, 0)
    add_into(0, 3, 0, (3, 4))
    to_mate[0].start()

    for k in (1, 3, 2):
        x_from(k).wait_recv()

    def h_copy(k):
        to = (z_hi + k) % 4
        return copy(h_send.at[to], h_recv.at[z_hi], h_s.at[to], h_r.at[z_hi], (d, to * 8 + plane))

    def h_from(k):
        to = (z_hi + k) % 4
        return copy(h_send.at[to], h_recv.at[to], h_s.at[to], h_r.at[to], (d, to * 8 + plane))

    def x_sum(to):
        rows = aligned(to, 32)
        total = x_own[rows, :]
        for k in (1, 2, 3):
            total = total + x_recv[x_device(k), rows, :].astype(F32)
        return total

    for k in (2, 1, 3):
        h_send[(z_hi + k) % 4] = x_sum((z_hi + k) % 4).astype(BF16)
        h_copy(k).start()
    h_own[...] = x_sum(z_hi)
    finish(0, 1)
    add_into(0, 3, 1, (2, 5))
    to_mate[1].start()
    combine(1)
    for k in (1, 3, 2):
        h_from(k).wait_recv()
    total = h_own[...]
    for k in (1, 2, 3):
        total = total + h_recv[(z_hi + k) % 4].astype(F32)
    d_send[...] = total.reshape(N_DP, 4, D)

    def d_copy(k):
        to = (d + k) % N_DP
        return copy(d_send.at[to], d_recv.at[d], d_s.at[to], d_r.at[d], (to, e))

    def d_from(k):
        to = (d + k) % N_DP
        return copy(d_send.at[to], d_recv.at[to], d_s.at[to], d_r.at[to], (to, e))

    loop(1, N_DP, lambda k: d_copy(k).start())

    for w, (out, others) in enumerate(((up_out, (3, 4)), (down_out, (2, 5)))):
        to_mate[w].wait_recv()
        finish(1, w)

        def piece(n):
            rows = aligned(n, 32)
            total = part[1, 3, w, rows, :].astype(F32)
            for slot in others:
                total = total + rs_recv[1, slot, rows, :].astype(F32)
            out[0, rows, :EARLY] = total[:, :EARLY].astype(BF16)
            out[0, rows, EARLY:] = (total[:, EARLY:] + z_recv[w, rows, :].astype(F32)).astype(BF16)

        loop(0, 4, piece)

    loop(1, N_DP, lambda k: d_from(k).wait_recv())
    total = d_send[d]
    for k in range(1, N_DP):
        total = total + d_recv[(d + k) % N_DP]
    enc_out[...] = total

    for hop in order:
        peers(hop, lambda h, k: to_g(h, k).wait_send())
        peers(hop, lambda h, k: to_n(h, k).wait_send())
        peers(hop, lambda g, k: give_back(g, k).wait_send())
    for p in range(2):
        for slot in range(6):
            rs(p, slot).wait_send()
    for w in range(2):
        to_mate[w].wait_send()
        for q in range(4):
            early(q, w).wait_send()
    to_core.wait_send()
    for k in (1, 2, 3):
        x_copy(k).wait_send()
        h_copy(k).wait_send()
    loop(1, N_DP, lambda k: d_copy(k).wait_send())


def settle(enc_in, up_in, down_in, enc_out, up_out, down_out):
    enc_out[...] = enc_in[...]
    up_out[...] = up_in[...]
    down_out[...] = down_in[...]


def body(cell_rows, cotangent, cluster_ids, enc_weight, up_weight, down_weight):
    vmem = pl.BlockSpec(memory_space=pltpu.VMEM)
    hbm = pl.BlockSpec(memory_space=pl.ANY)
    dma = pltpu.SemaphoreType.DMA
    outs = pl.pallas_call(
        kernel,
        name="step",
        out_shape=(
            jax.ShapeDtypeStruct((4, D), F32),
            jax.ShapeDtypeStruct((1, 128, H), BF16),
            jax.ShapeDtypeStruct((1, 128, H), BF16),
        ),
        in_specs=[vmem, vmem, vmem, hbm, hbm, hbm],
        out_specs=(vmem, vmem, vmem),
        scratch_shapes=[
            pltpu.VMEM((D, D), BF16),
            pltpu.VMEM((D, H), BF16),
            pltpu.VMEM((D, H), BF16),
            pltpu.VMEM((ROWS, H), F32),
            pltpu.VMEM((ALL_ROWS, D), BF16),
            pltpu.VMEM((SLOTS, D), BF16),
            pltpu.VMEM((SLOTS, D), BF16),
            pltpu.VMEM((SLOTS, D), BF16),
            pltpu.VMEM((SLOTS, D), BF16),
            pltpu.VMEM((SLOTS, H), BF16),
            pltpu.VMEM((SLOTS, H), BF16),
            pltpu.VMEM((SLOTS, D), BF16),
            pltpu.VMEM((SLOTS, D), BF16),
            pltpu.VMEM((ALL_ROWS, D), F32),
            pltpu.VMEM((ALL_ROWS, D), F32),
            pltpu.VMEM((ALL_ROWS, 128), F32),
            pltpu.VMEM((SLOTS, ALL_ROWS), BF16),
            pltpu.VMEM((ALL_ROWS, D), BF16),
            pltpu.VMEM((ALL_ROWS, D), BF16),
            pltpu.VMEM((2, 4, 2, 128, H), BF16),
            pltpu.VMEM((2, 6, 128, H), BF16),
            pltpu.VMEM((2, 128, H - EARLY), BF16),
            pltpu.VMEM((4, 2, 128, EARLY), BF16),
            pltpu.VMEM((512, D), F32),
            pltpu.VMEM((512, D), BF16),
            pltpu.VMEM((512, D), BF16),
            pltpu.VMEM((128, D), F32),
            pltpu.VMEM((4, 128, D), BF16),
            pltpu.VMEM((4, 128, D), BF16),
            pltpu.VMEM((32, D), F32),
            pltpu.VMEM((4, 32, D), BF16),
            pltpu.VMEM((4, 32, D), BF16),
            pltpu.VMEM((N_DP, 4, D), F32),
            pltpu.VMEM((N_DP, 4, D), F32),
            dma((3,)),
            dma((N_EX,)),
            dma((N_EX,)),
            dma((N_EX,)),
            dma((N_EX,)),
            dma((4, 2)),
            dma((4, 2)),
            dma((N_EX,)),
            dma((N_EX,)),
            dma((2, 6)),
            dma((2, 6)),
            dma((2,)),
            dma((2,)),
            dma((1,)),
            dma((1,)),
            dma((4,)),
            dma((4,)),
            dma((4,)),
            dma((4,)),
            dma((N_DP,)),
            dma((N_DP,)),
        ],
        compiler_params=pltpu.CompilerParams(
            collective_id=0, has_side_effects=True, vmem_limit_bytes=62 << 20
        ),
    )(
        cell_rows.reshape(ALL_ROWS, D),
        cotangent.reshape(ALL_ROWS, D),
        cluster_ids.reshape(MICRO, ROWS),
        enc_weight,
        up_weight,
        down_weight,
    )
    return pl.pallas_call(
        settle,
        name="settle",
        out_shape=tuple(jax.ShapeDtypeStruct(o.shape, o.dtype) for o in outs),
        in_specs=[vmem] * 3,
        out_specs=(vmem,) * 3,
    )(*outs)


def solution(mesh):
    in_specs = (
        P(None, ("dp", "expert"), None),
        P(None, ("dp", "expert"), None),
        P(None, ("dp", "expert"), None),
        P(),
        P("expert", None, None),
        P("expert", None, None),
    )
    out_specs = (P(("dp", "expert"), None), P("expert", "dp", None), P("expert", "dp", None))
    return jax.shard_map(body, mesh=mesh, in_specs=in_specs, out_specs=out_specs, check_vma=False)
```

```python
import jax
import jax.numpy as jnp
from jax import lax
from jax.experimental import pallas as pl
from jax.experimental.pallas import tpu as pltpu
from jax.sharding import PartitionSpec as P

MESH = pl.DeviceIdType.MESH
F32 = jnp.float32
BF16 = jnp.bfloat16
epsilon = 1e-06

N_DP = 8
N_EX = 32
D = 1024
H = 2048
ROWS = 128
MICRO = 2
ALL_ROWS = MICRO * ROWS
CAP = 8
SLOT = MICRO * CAP
SLOTS = N_EX * SLOT
WIDE = 512
EARLY = 384


def dot(a, b):
    return jnp.dot(a, b, preferred_element_type=F32)


def dot_nt(a, b):
    return lax.dot_general(a, b, (((1,), (1,)), ((), ())), preferred_element_type=F32)


def dot_tn(a, b):
    return lax.dot_general(a, b, (((0,), (0,)), ((), ())), preferred_element_type=F32)


def aligned(index, size):
    return pl.ds(pl.multiple_of(index * size, size), size)


def loop(low, high, step):
    def body(index, carry):
        step(index)
        return carry

    lax.fori_loop(low, high, body, 0)


def kernel(
    cell, cot, ids, encw_hbm, up_hbm, down_hbm,
    enc_out, up_out, down_out,
    encw, w_up, w_down, held, normed, send_n, send_g, recv_n, recv_g, pre_grad, active, back, ret,
    enc_s, slope_s, inv_s, placer, fperm, egrad,
    part, rs_recv, z_recv, early_recv,
    e_own, e_send, e_recv, x_own, x_send, x_recv, h_own, h_send, h_recv, d_send, d_recv,
    w_sem, disp_s, disp_r, dispg_s, dispg_r, early_s, early_r, ret_s, ret_r, rs_s, rs_r, z_s, z_r, c_s, c_r, x_s, x_r, h_s, h_r, d_s, d_r,
):
    d = lax.axis_index("dp")
    e = lax.axis_index("expert")
    z_lo, y = d // 4, d % 4
    z_hi, plane = e // 8, e % 8
    x, core = plane // 2, plane % 2
    right = (z_lo * 4 + (y + 1) % 4, e)
    left = (z_lo * 4 + (y + 3) % 4, e)
    mate = ((1 - z_lo) * 4 + y, e)

    def copy(src, dst, s, r, who):
        return pltpu.make_async_remote_copy(
            src_ref=src, dst_ref=dst, send_sem=s, recv_sem=r, device_id=who, device_id_type=MESH
        )

    enc_copy = pltpu.make_async_copy(encw_hbm, encw, w_sem.at[2])
    enc_copy.start()
    w_copies = [
        pltpu.make_async_copy(up_hbm.at[0], w_up, w_sem.at[0]),
        pltpu.make_async_copy(down_hbm.at[0], w_down, w_sem.at[1]),
    ]
    for item in w_copies:
        item.start()

    barrier = pltpu.get_barrier_semaphore()

    def greet_plane(k):
        index = z_lo * N_EX + e + k
        who = (((index // N_EX) % 2) * 4 + y, index % N_EX)
        pl.semaphore_signal(barrier, inc=1, device_id=who, device_id_type=MESH)

    def greet_ring(k):
        for half in range(2):
            who = (half * 4 + (y + k) % 4, e)
            pl.semaphore_signal(barrier, inc=1, device_id=who, device_id_type=MESH)

    loop(1, 2 * N_EX, greet_plane)
    loop(1, 4, greet_ring)

    upper = (
        lax.broadcasted_iota(jnp.int32, (ROWS, ROWS), 0) < lax.broadcasted_iota(jnp.int32, (ROWS, ROWS), 1)
    ).astype(F32).astype(BF16)
    for m in range(MICRO):
        label = ids[m : m + 1, :]
        onehot = (label == lax.broadcasted_iota(jnp.int32, (N_EX, ROWS), 0)).astype(F32)
        before = dot(onehot.astype(BF16), upper)
        rank = jnp.sum(before * onehot, axis=0, keepdims=True).astype(jnp.int32)
        target = label * SLOT + m * CAP + rank
        slots = lax.broadcasted_iota(jnp.int32, (SLOTS, ROWS), 0)
        placer[:, m * ROWS : (m + 1) * ROWS] = (slots == target).astype(F32).astype(BF16)

    def near(hop):
        return (z_lo, 0, 1 - z_lo, 1)[hop]

    def place(hop):
        group = (0, 1 + 2 * z_lo, 2, 1 + 2 * z_lo)[hop]
        return group * 8 + plane

    beside = (z_hi + 3 + 2 * z_lo) % 4

    def source(group, k):
        half, high = ((z_lo, z_hi), (0, beside), (1 - z_lo, (z_hi + 2) % 4), (1, beside))[group]
        other = (plane + k) % 8
        return group * 8 + other, (half * 4 + y, high * 8 + other)

    def target(hop, k):
        cluster = ((z_hi + hop) % 4) * 8 + (plane + k) % 8
        return cluster, (near(hop) * 4 + y, cluster)

    def sending(hop, k, src, dst, s, r):
        cluster, who = target(hop, k)
        at = place(hop)
        return copy(src.at[aligned(cluster, SLOT), :], dst.at[aligned(at, SLOT), :], s.at[cluster], r.at[at], who)

    def landing(group, k, src, dst, s, r):
        at, who = source(group, k)
        return copy(src.at[aligned(at, SLOT), :], dst.at[aligned(at, SLOT), :], s.at[at], r.at[at], who)

    def to_g(hop, k):
        return sending(hop, k, send_g, recv_g, dispg_s, dispg_r)

    def from_g(group, k):
        return landing(group, k, send_g, recv_g, dispg_s, dispg_r)

    def to_n(hop, k):
        return sending(hop, k, send_n, recv_n, disp_s, disp_r)

    def from_n(group, k):
        return landing(group, k, send_n, recv_n, disp_s, disp_r)

    def give_back(group, k):
        at, who = source(group, k)
        return copy(back.at[aligned(at, SLOT), :], ret.at[aligned(e, SLOT), :], ret_s.at[at], ret_r.at[e], who)

    def came_back(hop, k):
        cluster, who = target(hop, k)
        rows = aligned(cluster, SLOT)
        return copy(back.at[rows, :], ret.at[rows, :], ret_s.at[cluster], ret_r.at[cluster], who)

    order = (0, 1, 3, 2)
    far_first = (1, 3, 2, 0)

    def peers(index, step):
        loop(1 if index == 0 else 0, 8, lambda k: step(index, k))

    for hop in far_first:
        group = aligned((z_hi + hop) % 4, 128)
        send_g[group, :] = dot(placer[group, :], cot[...]).astype(BF16)
        if hop == far_first[0]:
            pl.semaphore_wait(barrier, 2 * N_EX - 1 + 6)
        peers(hop, lambda h, k: to_g(h, k).start())
    recv_g[aligned(plane, SLOT), :] = send_g[aligned(e, SLOT), :]

    inv_s[...] = jnp.zeros_like(inv_s)
    enc_copy.wait()

    def encode(n):
        cols = aligned(n, 256)
        pre = dot(cell[...], encw[:, cols])
        gate = jax.nn.sigmoid(pre)
        encoded = cell[:, cols].astype(F32) + pre * gate
        enc_s[:, cols] = encoded
        slope_s[:, cols] = gate * (1.0 + pre * (1.0 - gate))
        square = encoded * encoded
        inv_s[...] += square[:, :128] + square[:, 128:]

    loop(0, 4, encode)

    def normalize(i):
        rows = aligned(i, 64)
        inverse = lax.rsqrt(jnp.sum(inv_s[rows, :], axis=1, keepdims=True) * (1.0 / D) + epsilon)
        inv_s[rows, :] = jnp.broadcast_to(inverse, (64, 128))
        normed[rows, :] = (enc_s[rows, :] * inverse).astype(BF16)

    loop(0, 4, normalize)
    for hop in far_first:
        group = aligned((z_hi + hop) % 4, 128)
        send_n[group, :] = dot(placer[group, :], normed[...]).astype(BF16)
        peers(hop, lambda h, k: to_n(h, k).start())
    recv_n[aligned(plane, SLOT), :] = send_n[aligned(e, SLOT), :]

    def permute(n):
        row = lax.broadcasted_iota(jnp.int32, (256, 1), 0) + n * 256
        nat = (
            (row & 3)
            + (((row >> 2) & 7) << 7)
            + (((row >> 5) & 3) << 5)
            + (((row >> 7) & 3) << 3)
            + ((row >> 9) << 2)
        )
        pick = (lax.broadcasted_iota(jnp.int32, (256, D), 1) == nat).astype(F32).astype(BF16)
        fperm[aligned(n, 256), :] = dot_nt(pick, cell[...]).astype(BF16)

    loop(0, 4, permute)
    for item in w_copies:
        item.wait()

    def silu_and_grad(group, cols, act_grad):
        pre = dot(recv_n[group, :], w_up[:, cols])
        gate = jax.nn.sigmoid(pre)
        active[group, cols] = (pre * gate).astype(BF16)
        pre_grad[group, cols] = (act_grad * (gate * (1.0 + pre * (1.0 - gate)))).astype(BF16)

    def mlp(index):
        group = pl.ds(index * 128, 128)
        peers(index, lambda g, k: from_g(g, k).wait_recv())
        peers(index, lambda g, k: from_n(g, k).wait_recv())

        def hidden(n):
            cols = aligned(n, WIDE)
            silu_and_grad(group, cols, dot(recv_g[group, :], w_down[:, cols]))

        loop(0, H // WIDE, hidden)

    def mlp_last(index):
        group = pl.ds(index * 128, 128)
        peers(index, lambda g, k: from_g(g, k).wait_recv())

        def first(n):
            cols = aligned(n, WIDE)
            held[:, cols] = dot(recv_g[group, :], w_down[:, cols])

        loop(0, H // WIDE, first)
        peers(index, lambda g, k: from_n(g, k).wait_recv())
        for earlier in order[1:-1]:
            peers(earlier, lambda g, k: give_back(g, k).start())

        def hidden(n):
            cols = aligned(n, WIDE)
            silu_and_grad(group, cols, held[:, cols])

        loop(0, H // WIDE, hidden)

    def mlp_back(index):
        group = pl.ds(index * 128, 128)

        def backward(n):
            back[group, aligned(n, 256)] = dot_nt(pre_grad[group, :], w_up[aligned(n, 256), :]).astype(BF16)

        loop(0, D // 256, backward)

    for index in order[:-1]:
        mlp(index)
        mlp_back(index)
        if index == 0:
            peers(0, lambda g, k: give_back(g, k).start())
    mlp_last(order[-1])

    def grads(p, q):
        block = ((1 - z_lo) if p == 0 else z_lo) * 4 + (y + (2, 1, 3, 0)[q]) % 4
        up_t = recv_n[:, aligned(block, 128)].T
        down_t = recv_g[:, aligned(block, 128)].T

        def piece(n):
            cols = aligned(n, WIDE)
            part[p, q, 0, :, cols] = dot(up_t, pre_grad[:, cols]).astype(BF16)
            part[p, q, 1, :, cols] = dot(down_t, active[:, cols]).astype(BF16)

        loop(0, H // WIDE, piece)

    late = (pl.ds(EARLY, H - EARLY), pl.ds(0, H))

    def rs(p, slot):
        q, which, who = ((0, 0, right), (0, 1, left), (1, 1, right), (2, 0, left), (1, 0, right), (2, 1, left))[slot]
        return copy(
            part.at[p, q, which, :, late[p]], rs_recv.at[p, slot, :, late[p]], rs_s.at[p, slot], rs_r.at[p, slot], who
        )

    def early(q, w):
        return copy(
            part.at[0, q, w, :, pl.ds(0, EARLY)], early_recv.at[q, w], early_s.at[q, w], early_r.at[q, w], mate
        )

    def add_early(q):
        for w in range(2):
            early(q, w).wait_recv()

            def piece(n):
                rows = aligned(n, 64)
                total = part[1, q, w, rows, :EARLY].astype(F32) + early_recv[q, w, rows, :].astype(F32)
                part[1, q, w, rows, :EARLY] = total.astype(BF16)

            loop(0, 2, piece)

    def add_into(p, q, which, others):
        def piece(n):
            rows = aligned(n, 32)
            total = part[p, q, which, rows, late[p]].astype(F32)
            for slot in others:
                total = total + rs_recv[p, slot, rows, late[p]].astype(F32)
            part[p, q, which, rows, late[p]] = total.astype(BF16)

        loop(0, 4, piece)

    def combine(p):
        rs(p, 0).wait_recv()
        add_into(p, 1, 0, (0,))
        rs(p, 4).start()
        rs(p, 1).wait_recv()
        add_into(p, 2, 1, (1,))
        rs(p, 5).start()

    grads(0, 0)
    rs(0, 0).start()
    rs(0, 1).start()
    early(0, 0).start()
    early(0, 1).start()
    mlp_back(order[-1])
    peers(order[-1], lambda g, k: give_back(g, k).start())
    ret[aligned(e, SLOT), :] = back[aligned(plane, SLOT), :]
    for q in (1, 2, 3):
        grads(0, q)
        if q < 3:
            rs(0, q + 1).start()
        early(q, 0).start()
        early(q, 1).start()
    combine(0)
    grads(1, 0)
    add_early(0)
    rs(1, 0).start()
    rs(1, 1).start()
    for q in (1, 2, 3):
        grads(1, q)

    for hop in order:
        peers(hop, lambda h, k: came_back(h, k).wait_recv())

    def encoder_back(i):
        rows = aligned(i, 128)
        norm_grad = dot_tn(placer[:, rows], ret[...])
        encoded = enc_s[rows, :]
        inverse = inv_s[rows, 0:1]
        mean = jnp.sum(norm_grad * encoded, axis=1, keepdims=True) * (1.0 / D)
        grad = inverse * norm_grad - inverse * inverse * inverse * encoded * mean
        egrad[rows, :] = (grad * slope_s[rows, :]).astype(BF16)

    loop(0, 2, encoder_back)

    def enc_piece(index):
        return dot(fperm[aligned(index, 128), :], egrad[...])

    def enc_other(n):
        e_send[aligned(n, 128), :] = enc_piece((1 - core) * 4 + n).astype(BF16)

    def enc_own(n):
        e_own[aligned(n, 128), :] = enc_piece(core * 4 + n)

    loop(0, 4, enc_other)
    to_core = copy(e_send, e_recv, c_s.at[0], c_r.at[0], (d, e + 1 - 2 * core))
    to_core.start()
    loop(0, 4, enc_own)

    to_core.wait_recv()

    def x_device(k):
        return (x + k) % 4

    def x_copy(k):
        to = x_device(k)
        return copy(x_send.at[to], x_recv.at[x], x_s.at[to], x_r.at[x], (d, (z_hi * 4 + to) * 2 + core))

    def x_from(k):
        to = x_device(k)
        return copy(x_send.at[to], x_recv.at[to], x_s.at[to], x_r.at[to], (d, (z_hi * 4 + to) * 2 + core))

    for k in (2, 1, 3):
        rows = aligned(x_device(k), 128)
        x_send[x_device(k)] = (e_own[rows, :] + e_recv[rows, :].astype(F32)).astype(BF16)
        x_copy(k).start()
    rows = aligned(x, 128)
    x_own[...] = e_own[rows, :] + e_recv[rows, :].astype(F32)

    add_early(1)
    rs(1, 2).start()
    add_early(2)
    rs(1, 3).start()

    def finish(p, w):
        for slot in ((3, 4), (2, 5))[w]:
            rs(p, slot).wait_recv()

    to_mate = [
        copy(part.at[0, 3, w, :, late[0]], z_recv.at[w], z_s.at[w], z_r.at[w], mate) for w in range(2)
    ]
    finish(0, 0)
    add_into(0, 3, 0, (3, 4))
    to_mate[0].start()
    combine(1)

    for k in (1, 3, 2):
        x_from(k).wait_recv()

    def h_copy(k):
        to = (z_hi + k) % 4
        return copy(h_send.at[to], h_recv.at[z_hi], h_s.at[to], h_r.at[z_hi], (d, to * 8 + plane))

    def h_from(k):
        to = (z_hi + k) % 4
        return copy(h_send.at[to], h_recv.at[to], h_s.at[to], h_r.at[to], (d, to * 8 + plane))

    def x_sum(to):
        rows = aligned(to, 32)
        total = x_own[rows, :]
        for k in (1, 2, 3):
            total = total + x_recv[x_device(k), rows, :].astype(F32)
        return total

    for k in (2, 1, 3):
        h_send[(z_hi + k) % 4] = x_sum((z_hi + k) % 4).astype(BF16)
        h_copy(k).start()
    h_own[...] = x_sum(z_hi)
    finish(0, 1)
    add_into(0, 3, 1, (2, 5))
    to_mate[1].start()
    for k in (1, 3, 2):
        h_from(k).wait_recv()
    total = h_own[...]
    for k in (1, 2, 3):
        total = total + h_recv[(z_hi + k) % 4].astype(F32)
    d_send[...] = total.reshape(N_DP, 4, D)

    def d_copy(k):
        to = (d + k) % N_DP
        return copy(d_send.at[to], d_recv.at[d], d_s.at[to], d_r.at[d], (to, e))

    def d_from(k):
        to = (d + k) % N_DP
        return copy(d_send.at[to], d_recv.at[to], d_s.at[to], d_r.at[to], (to, e))

    loop(1, N_DP, lambda k: d_copy(k).start())

    for w, (out, others) in enumerate(((up_out, (3, 4)), (down_out, (2, 5)))):
        early(3, w).wait_recv()
        to_mate[w].wait_recv()
        finish(1, w)

        def piece(n):
            rows = aligned(n, 32)
            total = part[1, 3, w, rows, :].astype(F32)
            for slot in others:
                total = total + rs_recv[1, slot, rows, :].astype(F32)
            out[0, rows, :EARLY] = (total[:, :EARLY] + early_recv[3, w, rows, :].astype(F32)).astype(BF16)
            out[0, rows, EARLY:] = (total[:, EARLY:] + z_recv[w, rows, :].astype(F32)).astype(BF16)

        loop(0, 4, piece)

    loop(1, N_DP, lambda k: d_from(k).wait_recv())
    total = d_send[d]
    for k in range(1, N_DP):
        total = total + d_recv[(d + k) % N_DP]
    enc_out[...] = total

    for hop in order:
        peers(hop, lambda h, k: to_g(h, k).wait_send())
        peers(hop, lambda h, k: to_n(h, k).wait_send())
        peers(hop, lambda g, k: give_back(g, k).wait_send())
    for p in range(2):
        for slot in range(6):
            rs(p, slot).wait_send()
    for w in range(2):
        to_mate[w].wait_send()
        for q in range(4):
            early(q, w).wait_send()
    to_core.wait_send()
    for k in (1, 2, 3):
        x_copy(k).wait_send()
        h_copy(k).wait_send()
    loop(1, N_DP, lambda k: d_copy(k).wait_send())


def settle(enc_in, up_in, down_in, enc_out, up_out, down_out):
    enc_out[...] = enc_in[...]
    up_out[...] = up_in[...]
    down_out[...] = down_in[...]


def body(cell_rows, cotangent, cluster_ids, enc_weight, up_weight, down_weight):
    vmem = pl.BlockSpec(memory_space=pltpu.VMEM)
    hbm = pl.BlockSpec(memory_space=pl.ANY)
    dma = pltpu.SemaphoreType.DMA
    outs = pl.pallas_call(
        kernel,
        name="step",
        out_shape=(
            jax.ShapeDtypeStruct((4, D), F32),
            jax.ShapeDtypeStruct((1, 128, H), BF16),
            jax.ShapeDtypeStruct((1, 128, H), BF16),
        ),
        in_specs=[vmem, vmem, vmem, hbm, hbm, hbm],
        out_specs=(vmem, vmem, vmem),
        scratch_shapes=[
            pltpu.VMEM((D, D), BF16),
            pltpu.VMEM((D, H), BF16),
            pltpu.VMEM((D, H), BF16),
            pltpu.VMEM((ROWS, H), F32),
            pltpu.VMEM((ALL_ROWS, D), BF16),
            pltpu.VMEM((SLOTS, D), BF16),
            pltpu.VMEM((SLOTS, D), BF16),
            pltpu.VMEM((SLOTS, D), BF16),
            pltpu.VMEM((SLOTS, D), BF16),
            pltpu.VMEM((SLOTS, H), BF16),
            pltpu.VMEM((SLOTS, H), BF16),
            pltpu.VMEM((SLOTS, D), BF16),
            pltpu.VMEM((SLOTS, D), BF16),
            pltpu.VMEM((ALL_ROWS, D), F32),
            pltpu.VMEM((ALL_ROWS, D), F32),
            pltpu.VMEM((ALL_ROWS, 128), F32),
            pltpu.VMEM((SLOTS, ALL_ROWS), BF16),
            pltpu.VMEM((D, ALL_ROWS), BF16),
            pltpu.VMEM((ALL_ROWS, D), BF16),
            pltpu.VMEM((2, 4, 2, 128, H), BF16),
            pltpu.VMEM((2, 6, 128, H), BF16),
            pltpu.VMEM((2, 128, H - EARLY), BF16),
            pltpu.VMEM((4, 2, 128, EARLY), BF16),
            pltpu.VMEM((512, D), F32),
            pltpu.VMEM((512, D), BF16),
            pltpu.VMEM((512, D), BF16),
            pltpu.VMEM((128, D), F32),
            pltpu.VMEM((4, 128, D), BF16),
            pltpu.VMEM((4, 128, D), BF16),
            pltpu.VMEM((32, D), F32),
            pltpu.VMEM((4, 32, D), BF16),
            pltpu.VMEM((4, 32, D), BF16),
            pltpu.VMEM((N_DP, 4, D), F32),
            pltpu.VMEM((N_DP, 4, D), F32),
            dma((3,)),
            dma((N_EX,)),
            dma((N_EX,)),
            dma((N_EX,)),
            dma((N_EX,)),
            dma((4, 2)),
            dma((4, 2)),
            dma((N_EX,)),
            dma((N_EX,)),
            dma((2, 6)),
            dma((2, 6)),
            dma((2,)),
            dma((2,)),
            dma((1,)),
            dma((1,)),
            dma((4,)),
            dma((4,)),
            dma((4,)),
            dma((4,)),
            dma((N_DP,)),
            dma((N_DP,)),
        ],
        compiler_params=pltpu.CompilerParams(
            collective_id=0, has_side_effects=True, vmem_limit_bytes=62 << 20
        ),
    )(
        cell_rows.reshape(ALL_ROWS, D),
        cotangent.reshape(ALL_ROWS, D),
        cluster_ids.reshape(MICRO, ROWS),
        enc_weight,
        up_weight,
        down_weight,
    )
    return pl.pallas_call(
        settle,
        name="settle",
        out_shape=tuple(jax.ShapeDtypeStruct(o.shape, o.dtype) for o in outs),
        in_specs=[vmem] * 3,
        out_specs=(vmem,) * 3,
    )(*outs)


def solution(mesh):
    in_specs = (
        P(None, ("dp", "expert"), None),
        P(None, ("dp", "expert"), None),
        P(None, ("dp", "expert"), None),
        P(),
        P("expert", None, None),
        P("expert", None, None),
    )
    out_specs = (P(("dp", "expert"), None), P("expert", "dp", None), P("expert", "dp", None))
    return jax.shard_map(body, mesh=mesh, in_specs=in_specs, out_specs=out_specs, check_vma=False)
```

```python
import jax
import jax.numpy as jnp
from jax import lax
from jax.experimental import pallas as pl
from jax.experimental.pallas import tpu as pltpu
from jax.sharding import PartitionSpec as P

MESH = pl.DeviceIdType.MESH
F32 = jnp.float32
BF16 = jnp.bfloat16
epsilon = 1e-06

N_DP = 8
N_EX = 32
D = 1024
H = 2048
ROWS = 128
MICRO = 2
ALL_ROWS = MICRO * ROWS
CAP = 8
SLOT = MICRO * CAP
SLOTS = N_EX * SLOT
WIDE = 512
EARLY = 640


def dot(a, b):
    return jnp.dot(a, b, preferred_element_type=F32)


def dot_nt(a, b):
    return lax.dot_general(a, b, (((1,), (1,)), ((), ())), preferred_element_type=F32)


def dot_tn(a, b):
    return lax.dot_general(a, b, (((0,), (0,)), ((), ())), preferred_element_type=F32)


def aligned(index, size):
    return pl.ds(pl.multiple_of(index * size, size), size)


def loop(low, high, step):
    def body(index, carry):
        step(index)
        return carry

    lax.fori_loop(low, high, body, 0)


def kernel(
    cell, cot, ids, encw_hbm, up_hbm, down_hbm,
    enc_out, up_out, down_out,
    encw, w_up, w_down, held, normed, send_n, send_g, recv_n, recv_g, pre_grad, active, back, ret,
    enc_s, slope_s, inv_s, placer, fperm, egrad,
    part, rs_recv, z_recv, early_recv,
    e_own, e_send, e_recv, x_own, x_send, x_recv, h_own, h_send, h_recv, d_send, d_recv,
    w_sem, disp_s, disp_r, dispg_s, dispg_r, early_s, early_r, ret_s, ret_r, rs_s, rs_r, z_s, z_r, c_s, c_r, x_s, x_r, h_s, h_r, d_s, d_r,
):
    d = lax.axis_index("dp")
    e = lax.axis_index("expert")
    z_lo, y = d // 4, d % 4
    z_hi, plane = e // 8, e % 8
    x, core = plane // 2, plane % 2
    right = (z_lo * 4 + (y + 1) % 4, e)
    left = (z_lo * 4 + (y + 3) % 4, e)
    mate = ((1 - z_lo) * 4 + y, e)

    def copy(src, dst, s, r, who):
        return pltpu.make_async_remote_copy(
            src_ref=src, dst_ref=dst, send_sem=s, recv_sem=r, device_id=who, device_id_type=MESH
        )

    enc_copy = pltpu.make_async_copy(encw_hbm, encw, w_sem.at[2])
    enc_copy.start()
    w_copies = [
        pltpu.make_async_copy(up_hbm.at[0], w_up, w_sem.at[0]),
        pltpu.make_async_copy(down_hbm.at[0], w_down, w_sem.at[1]),
    ]
    for item in w_copies:
        item.start()

    barrier = pltpu.get_barrier_semaphore()

    def greet_plane(k):
        index = z_lo * N_EX + e + k
        who = (((index // N_EX) % 2) * 4 + y, index % N_EX)
        pl.semaphore_signal(barrier, inc=1, device_id=who, device_id_type=MESH)

    def greet_ring(k):
        for half in range(2):
            who = (half * 4 + (y + k) % 4, e)
            pl.semaphore_signal(barrier, inc=1, device_id=who, device_id_type=MESH)

    loop(1, 2 * N_EX, greet_plane)
    loop(1, 4, greet_ring)

    upper = (
        lax.broadcasted_iota(jnp.int32, (ROWS, ROWS), 0) < lax.broadcasted_iota(jnp.int32, (ROWS, ROWS), 1)
    ).astype(F32).astype(BF16)
    for m in range(MICRO):
        label = ids[m : m + 1, :]
        onehot = (label == lax.broadcasted_iota(jnp.int32, (N_EX, ROWS), 0)).astype(F32)
        before = dot(onehot.astype(BF16), upper)
        rank = jnp.sum(before * onehot, axis=0, keepdims=True).astype(jnp.int32)
        target = label * SLOT + m * CAP + rank
        slots = lax.broadcasted_iota(jnp.int32, (SLOTS, ROWS), 0)
        placer[:, m * ROWS : (m + 1) * ROWS] = (slots == target).astype(F32).astype(BF16)

    def near(hop):
        return (z_lo, 0, 1 - z_lo, 1)[hop]

    def place(hop):
        group = (0, 1 + 2 * z_lo, 2, 1 + 2 * z_lo)[hop]
        return group * 8 + plane

    beside = (z_hi + 3 + 2 * z_lo) % 4

    def source(group, k):
        half, high = ((z_lo, z_hi), (0, beside), (1 - z_lo, (z_hi + 2) % 4), (1, beside))[group]
        other = (plane + k) % 8
        return group * 8 + other, (half * 4 + y, high * 8 + other)

    def target(hop, k):
        cluster = ((z_hi + hop) % 4) * 8 + (plane + k) % 8
        return cluster, (near(hop) * 4 + y, cluster)

    def sending(hop, k, src, dst, s, r):
        cluster, who = target(hop, k)
        at = place(hop)
        return copy(src.at[aligned(cluster, SLOT), :], dst.at[aligned(at, SLOT), :], s.at[cluster], r.at[at], who)

    def landing(group, k, src, dst, s, r):
        at, who = source(group, k)
        return copy(src.at[aligned(at, SLOT), :], dst.at[aligned(at, SLOT), :], s.at[at], r.at[at], who)

    def to_g(hop, k):
        return sending(hop, k, send_g, recv_g, dispg_s, dispg_r)

    def from_g(group, k):
        return landing(group, k, send_g, recv_g, dispg_s, dispg_r)

    def to_n(hop, k):
        return sending(hop, k, send_n, recv_n, disp_s, disp_r)

    def from_n(group, k):
        return landing(group, k, send_n, recv_n, disp_s, disp_r)

    def give_back(group, k):
        at, who = source(group, k)
        return copy(back.at[aligned(at, SLOT), :], ret.at[aligned(e, SLOT), :], ret_s.at[at], ret_r.at[e], who)

    def came_back(hop, k):
        cluster, who = target(hop, k)
        rows = aligned(cluster, SLOT)
        return copy(back.at[rows, :], ret.at[rows, :], ret_s.at[cluster], ret_r.at[cluster], who)

    order = (0, 1, 3, 2)
    far_first = (1, 3, 2, 0)

    def peers(index, step):
        loop(1 if index == 0 else 0, 8, lambda k: step(index, k))

    for hop in far_first:
        group = aligned((z_hi + hop) % 4, 128)
        send_g[group, :] = dot(placer[group, :], cot[...]).astype(BF16)
        if hop == far_first[0]:
            pl.semaphore_wait(barrier, 2 * N_EX - 1 + 6)
        peers(hop, lambda h, k: to_g(h, k).start())
    recv_g[aligned(plane, SLOT), :] = send_g[aligned(e, SLOT), :]

    inv_s[...] = jnp.zeros_like(inv_s)
    enc_copy.wait()

    def encode(n):
        cols = aligned(n, 256)
        pre = dot(cell[...], encw[:, cols])
        gate = jax.nn.sigmoid(pre)
        encoded = cell[:, cols].astype(F32) + pre * gate
        enc_s[:, cols] = encoded
        slope_s[:, cols] = gate * (1.0 + pre * (1.0 - gate))
        square = encoded * encoded
        inv_s[...] += square[:, :128] + square[:, 128:]

    loop(0, 4, encode)

    def normalize(i):
        rows = aligned(i, 64)
        inverse = lax.rsqrt(jnp.sum(inv_s[rows, :], axis=1, keepdims=True) * (1.0 / D) + epsilon)
        inv_s[rows, :] = jnp.broadcast_to(inverse, (64, 128))
        normed[rows, :] = (enc_s[rows, :] * inverse).astype(BF16)

    loop(0, 4, normalize)
    for hop in far_first:
        group = aligned((z_hi + hop) % 4, 128)
        send_n[group, :] = dot(placer[group, :], normed[...]).astype(BF16)
        peers(hop, lambda h, k: to_n(h, k).start())
    recv_n[aligned(plane, SLOT), :] = send_n[aligned(e, SLOT), :]

    def permute(n):
        row = lax.broadcasted_iota(jnp.int32, (256, 1), 0) + n * 256
        nat = (
            (row & 3)
            + (((row >> 2) & 7) << 7)
            + (((row >> 5) & 3) << 5)
            + (((row >> 7) & 3) << 3)
            + ((row >> 9) << 2)
        )
        pick = (lax.broadcasted_iota(jnp.int32, (256, D), 1) == nat).astype(F32).astype(BF16)
        fperm[aligned(n, 256), :] = dot_nt(pick, cell[...]).astype(BF16)

    loop(0, 4, permute)
    for item in w_copies:
        item.wait()

    def silu_and_grad(group, cols, act_grad):
        pre = dot(recv_n[group, :], w_up[:, cols])
        gate = jax.nn.sigmoid(pre)
        active[group, cols] = (pre * gate).astype(BF16)
        pre_grad[group, cols] = (act_grad * (gate * (1.0 + pre * (1.0 - gate)))).astype(BF16)

    def mlp(index):
        group = pl.ds(index * 128, 128)
        peers(index, lambda g, k: from_g(g, k).wait_recv())
        peers(index, lambda g, k: from_n(g, k).wait_recv())

        def hidden(n):
            cols = aligned(n, WIDE)
            silu_and_grad(group, cols, dot(recv_g[group, :], w_down[:, cols]))

        loop(0, H // WIDE, hidden)

    def mlp_last(index):
        group = pl.ds(index * 128, 128)
        peers(index, lambda g, k: from_g(g, k).wait_recv())

        def first(n):
            cols = aligned(n, WIDE)
            held[:, cols] = dot(recv_g[group, :], w_down[:, cols])

        loop(0, H // WIDE, first)
        peers(index, lambda g, k: from_n(g, k).wait_recv())
        for earlier in order[1:-1]:
            peers(earlier, lambda g, k: give_back(g, k).start())

        def hidden(n):
            cols = aligned(n, WIDE)
            silu_and_grad(group, cols, held[:, cols])

        loop(0, H // WIDE, hidden)

    def mlp_back(index):
        group = pl.ds(index * 128, 128)

        def backward(n):
            back[group, aligned(n, 256)] = dot_nt(pre_grad[group, :], w_up[aligned(n, 256), :]).astype(BF16)

        loop(0, D // 256, backward)

    for index in order[:-1]:
        mlp(index)
        mlp_back(index)
        if index == 0:
            peers(0, lambda g, k: give_back(g, k).start())
    mlp_last(order[-1])

    def grads(p, q):
        block = ((1 - z_lo) if p == 0 else z_lo) * 4 + (y + (2, 1, 3, 0)[q]) % 4
        up_t = recv_n[:, aligned(block, 128)].T
        down_t = recv_g[:, aligned(block, 128)].T

        def piece(n):
            cols = aligned(n, WIDE)
            part[p, q, 0, :, cols] = dot(up_t, pre_grad[:, cols]).astype(BF16)
            part[p, q, 1, :, cols] = dot(down_t, active[:, cols]).astype(BF16)

        loop(0, H // WIDE, piece)

    late = (pl.ds(EARLY, H - EARLY), pl.ds(0, H))

    def rs(p, slot):
        q, which, who = ((0, 0, right), (0, 1, left), (1, 1, right), (2, 0, left), (1, 0, right), (2, 1, left))[slot]
        return copy(
            part.at[p, q, which, :, late[p]], rs_recv.at[p, slot, :, late[p]], rs_s.at[p, slot], rs_r.at[p, slot], who
        )

    def early(q, w):
        return copy(
            part.at[0, q, w, :, pl.ds(0, EARLY)], early_recv.at[q, w], early_s.at[q, w], early_r.at[q, w], mate
        )

    def add_early(q):
        for w in range(2):
            early(q, w).wait_recv()

            def piece(n):
                rows = aligned(n, 64)
                total = part[1, q, w, rows, :EARLY].astype(F32) + early_recv[q, w, rows, :].astype(F32)
                part[1, q, w, rows, :EARLY] = total.astype(BF16)

            loop(0, 2, piece)

    def add_into(p, q, which, others):
        def piece(n):
            rows = aligned(n, 32)
            total = part[p, q, which, rows, late[p]].astype(F32)
            for slot in others:
                total = total + rs_recv[p, slot, rows, late[p]].astype(F32)
            part[p, q, which, rows, late[p]] = total.astype(BF16)

        loop(0, 4, piece)

    def combine(p):
        rs(p, 0).wait_recv()
        add_into(p, 1, 0, (0,))
        rs(p, 4).start()
        rs(p, 1).wait_recv()
        add_into(p, 2, 1, (1,))
        rs(p, 5).start()

    grads(0, 0)
    rs(0, 0).start()
    rs(0, 1).start()
    early(0, 0).start()
    early(0, 1).start()
    mlp_back(order[-1])
    peers(order[-1], lambda g, k: give_back(g, k).start())
    ret[aligned(e, SLOT), :] = back[aligned(plane, SLOT), :]
    for q in (1, 2, 3):
        grads(0, q)
        if q < 3:
            rs(0, q + 1).start()
        early(q, 0).start()
        early(q, 1).start()
    combine(0)
    grads(1, 0)
    add_early(0)
    rs(1, 0).start()
    rs(1, 1).start()
    for q in (1, 2, 3):
        grads(1, q)

    for hop in order:
        peers(hop, lambda h, k: came_back(h, k).wait_recv())

    def encoder_back(i):
        rows = aligned(i, 128)
        norm_grad = dot_tn(placer[:, rows], ret[...])
        encoded = enc_s[rows, :]
        inverse = inv_s[rows, 0:1]
        mean = jnp.sum(norm_grad * encoded, axis=1, keepdims=True) * (1.0 / D)
        grad = inverse * norm_grad - inverse * inverse * inverse * encoded * mean
        egrad[rows, :] = (grad * slope_s[rows, :]).astype(BF16)

    loop(0, 2, encoder_back)

    def enc_piece(index):
        return dot(fperm[aligned(index, 128), :], egrad[...])

    def enc_other(n):
        e_send[aligned(n, 128), :] = enc_piece((1 - core) * 4 + n).astype(BF16)

    def enc_own(n):
        e_own[aligned(n, 128), :] = enc_piece(core * 4 + n)

    loop(0, 4, enc_other)
    to_core = copy(e_send, e_recv, c_s.at[0], c_r.at[0], (d, e + 1 - 2 * core))
    to_core.start()
    loop(0, 4, enc_own)

    to_core.wait_recv()

    def x_device(k):
        return (x + k) % 4

    def x_copy(k):
        to = x_device(k)
        return copy(x_send.at[to], x_recv.at[x], x_s.at[to], x_r.at[x], (d, (z_hi * 4 + to) * 2 + core))

    def x_from(k):
        to = x_device(k)
        return copy(x_send.at[to], x_recv.at[to], x_s.at[to], x_r.at[to], (d, (z_hi * 4 + to) * 2 + core))

    for k in (2, 1, 3):
        rows = aligned(x_device(k), 128)
        x_send[x_device(k)] = (e_own[rows, :] + e_recv[rows, :].astype(F32)).astype(BF16)
        x_copy(k).start()
    rows = aligned(x, 128)
    x_own[...] = e_own[rows, :] + e_recv[rows, :].astype(F32)

    add_early(1)
    rs(1, 2).start()
    add_early(2)
    rs(1, 3).start()

    def finish(p, w):
        for slot in ((3, 4), (2, 5))[w]:
            rs(p, slot).wait_recv()

    to_mate = [
        copy(part.at[0, 3, w, :, late[0]], z_recv.at[w], z_s.at[w], z_r.at[w], mate) for w in range(2)
    ]
    finish(0, 0)
    add_into(0, 3, 0, (3, 4))
    to_mate[0].start()
    combine(1)

    for k in (1, 3, 2):
        x_from(k).wait_recv()

    def h_copy(k):
        to = (z_hi + k) % 4
        return copy(h_send.at[to], h_recv.at[z_hi], h_s.at[to], h_r.at[z_hi], (d, to * 8 + plane))

    def h_from(k):
        to = (z_hi + k) % 4
        return copy(h_send.at[to], h_recv.at[to], h_s.at[to], h_r.at[to], (d, to * 8 + plane))

    def x_sum(to):
        rows = aligned(to, 32)
        total = x_own[rows, :]
        for k in (1, 2, 3):
            total = total + x_recv[x_device(k), rows, :].astype(F32)
        return total

    for k in (2, 1, 3):
        h_send[(z_hi + k) % 4] = x_sum((z_hi + k) % 4).astype(BF16)
        h_copy(k).start()
    h_own[...] = x_sum(z_hi)
    finish(0, 1)
    add_into(0, 3, 1, (2, 5))
    to_mate[1].start()
    for k in (1, 3, 2):
        h_from(k).wait_recv()
    total = h_own[...]
    for k in (1, 2, 3):
        total = total + h_recv[(z_hi + k) % 4].astype(F32)
    d_send[...] = total.reshape(N_DP, 4, D)

    def d_copy(k):
        to = (d + k) % N_DP
        return copy(d_send.at[to], d_recv.at[d], d_s.at[to], d_r.at[d], (to, e))

    def d_from(k):
        to = (d + k) % N_DP
        return copy(d_send.at[to], d_recv.at[to], d_s.at[to], d_r.at[to], (to, e))

    loop(1, N_DP, lambda k: d_copy(k).start())

    for w, (out, others) in enumerate(((up_out, (3, 4)), (down_out, (2, 5)))):
        early(3, w).wait_recv()
        to_mate[w].wait_recv()
        finish(1, w)

        def piece(n):
            rows = aligned(n, 32)
            total = part[1, 3, w, rows, :].astype(F32)
            for slot in others:
                total = total + rs_recv[1, slot, rows, :].astype(F32)
            out[0, rows, :EARLY] = (total[:, :EARLY] + early_recv[3, w, rows, :].astype(F32)).astype(BF16)
            out[0, rows, EARLY:] = (total[:, EARLY:] + z_recv[w, rows, :].astype(F32)).astype(BF16)

        loop(0, 4, piece)

    loop(1, N_DP, lambda k: d_from(k).wait_recv())
    total = d_send[d]
    for k in range(1, N_DP):
        total = total + d_recv[(d + k) % N_DP]
    enc_out[...] = total

    for hop in order:
        peers(hop, lambda h, k: to_g(h, k).wait_send())
        peers(hop, lambda h, k: to_n(h, k).wait_send())
        peers(hop, lambda g, k: give_back(g, k).wait_send())
    for p in range(2):
        for slot in range(6):
            rs(p, slot).wait_send()
    for w in range(2):
        to_mate[w].wait_send()
        for q in range(4):
            early(q, w).wait_send()
    to_core.wait_send()
    for k in (1, 2, 3):
        x_copy(k).wait_send()
        h_copy(k).wait_send()
    loop(1, N_DP, lambda k: d_copy(k).wait_send())


def settle(enc_in, up_in, down_in, enc_out, up_out, down_out):
    enc_out[...] = enc_in[...]
    up_out[...] = up_in[...]
    down_out[...] = down_in[...]


def body(cell_rows, cotangent, cluster_ids, enc_weight, up_weight, down_weight):
    vmem = pl.BlockSpec(memory_space=pltpu.VMEM)
    hbm = pl.BlockSpec(memory_space=pl.ANY)
    dma = pltpu.SemaphoreType.DMA
    outs = pl.pallas_call(
        kernel,
        name="step",
        out_shape=(
            jax.ShapeDtypeStruct((4, D), F32),
            jax.ShapeDtypeStruct((1, 128, H), BF16),
            jax.ShapeDtypeStruct((1, 128, H), BF16),
        ),
        in_specs=[vmem, vmem, vmem, hbm, hbm, hbm],
        out_specs=(vmem, vmem, vmem),
        scratch_shapes=[
            pltpu.VMEM((D, D), BF16),
            pltpu.VMEM((D, H), BF16),
            pltpu.VMEM((D, H), BF16),
            pltpu.VMEM((ROWS, H), F32),
            pltpu.VMEM((ALL_ROWS, D), BF16),
            pltpu.VMEM((SLOTS, D), BF16),
            pltpu.VMEM((SLOTS, D), BF16),
            pltpu.VMEM((SLOTS, D), BF16),
            pltpu.VMEM((SLOTS, D), BF16),
            pltpu.VMEM((SLOTS, H), BF16),
            pltpu.VMEM((SLOTS, H), BF16),
            pltpu.VMEM((SLOTS, D), BF16),
            pltpu.VMEM((SLOTS, D), BF16),
            pltpu.VMEM((ALL_ROWS, D), F32),
            pltpu.VMEM((ALL_ROWS, D), F32),
            pltpu.VMEM((ALL_ROWS, 128), F32),
            pltpu.VMEM((SLOTS, ALL_ROWS), BF16),
            pltpu.VMEM((D, ALL_ROWS), BF16),
            pltpu.VMEM((ALL_ROWS, D), BF16),
            pltpu.VMEM((2, 4, 2, 128, H), BF16),
            pltpu.VMEM((2, 6, 128, H), BF16),
            pltpu.VMEM((2, 128, H - EARLY), BF16),
            pltpu.VMEM((4, 2, 128, EARLY), BF16),
            pltpu.VMEM((512, D), F32),
            pltpu.VMEM((512, D), BF16),
            pltpu.VMEM((512, D), BF16),
            pltpu.VMEM((128, D), F32),
            pltpu.VMEM((4, 128, D), BF16),
            pltpu.VMEM((4, 128, D), BF16),
            pltpu.VMEM((32, D), F32),
            pltpu.VMEM((4, 32, D), BF16),
            pltpu.VMEM((4, 32, D), BF16),
            pltpu.VMEM((N_DP, 4, D), F32),
            pltpu.VMEM((N_DP, 4, D), F32),
            dma((3,)),
            dma((N_EX,)),
            dma((N_EX,)),
            dma((N_EX,)),
            dma((N_EX,)),
            dma((4, 2)),
            dma((4, 2)),
            dma((N_EX,)),
            dma((N_EX,)),
            dma((2, 6)),
            dma((2, 6)),
            dma((2,)),
            dma((2,)),
            dma((1,)),
            dma((1,)),
            dma((4,)),
            dma((4,)),
            dma((4,)),
            dma((4,)),
            dma((N_DP,)),
            dma((N_DP,)),
        ],
        compiler_params=pltpu.CompilerParams(
            collective_id=0, has_side_effects=True, vmem_limit_bytes=62 << 20
        ),
    )(
        cell_rows.reshape(ALL_ROWS, D),
        cotangent.reshape(ALL_ROWS, D),
        cluster_ids.reshape(MICRO, ROWS),
        enc_weight,
        up_weight,
        down_weight,
    )
    return pl.pallas_call(
        settle,
        name="settle",
        out_shape=tuple(jax.ShapeDtypeStruct(o.shape, o.dtype) for o in outs),
        in_specs=[vmem] * 3,
        out_specs=(vmem,) * 3,
    )(*outs)


def solution(mesh):
    in_specs = (
        P(None, ("dp", "expert"), None),
        P(None, ("dp", "expert"), None),
        P(None, ("dp", "expert"), None),
        P(),
        P("expert", None, None),
        P("expert", None, None),
    )
    out_specs = (P(("dp", "expert"), None), P("expert", "dp", None), P("expert", "dp", None))
    return jax.shard_map(body, mesh=mesh, in_specs=in_specs, out_specs=out_specs, check_vma=False)
```
